256 devices in a mesh: wide: 32 (over y_lo, z, core), narrow: 8 (over y_hi, x).
Axes of the slice: x: 4, y: 4 (y_hi: 2, y_lo: 2; y = y_hi * 2 + y_lo), z: 8, core: 2. Of those that a mesh axis runs over, the one named last changes fastest.
Arguments:
- vectors: bfloat16 [65536, 768], P(('wide', 'narrow')), may hold values from -15 to 15
- block_sides: int32 [512], P(('wide', 'narrow')), may hold values from 0 to 1, as said below
- centers: bfloat16 [32768, 768], P(('wide', 'narrow')), may hold values from -8.5 to 8.5
Outputs:
- new_centers: bfloat16 [32768, 768], P(('wide', 'narrow'))
The draws below stay inside these ranges and needn't reach their ends.
Inputs may be any that keep to these rules, and one draw needn't show every extreme that they name: `block_sides`: of the 2 labels of one device (consecutive runs of 2 entries), exactly half are 1.
All inputs are finite; a program needn't handle non-finite values.
Results may differ from the reference program's by a relative error of at most 0.0018.
The reference program's roundings to bfloat16 on the way count: a program that leaves them out, or rounds other values in their place, can miss the bound.
Values may be sent and summed in bfloat16 or wider, within the bound.
A program may use at most 64 MiB of HBM per device.

```python
import math
import jax
import jax.numpy as jnp
from jax import lax

D = 768
KS = 128
VEC_DEV = 256
BLK = 128
LEVEL = 1
ITERS = 2
GROUPS = 4
LOOP = 8
K = 8192
BLK_DEV = 2
VECTORS = 65536
BLOCKS = 512
N_WIDE = 32
N_NARROW = 8


def draw_vectors(key, part):
    noise = jnp.clip(jax.random.normal(jax.random.fold_in(key, 1), (VECTORS, D), jnp.float32), -5.0, 5.0)
    scales = jnp.exp(jax.random.uniform(jax.random.fold_in(key, 3), (VECTORS, 1), jnp.float32, math.log(0.5), math.log(2.0)))
    values = scales * noise
    return values.astype(jnp.bfloat16)


def draw_centers(key, part):
    noise = jnp.clip(jax.random.normal(jax.random.fold_in(key, 4), (GROUPS * K, D), jnp.float32), -4.0, 4.0)
    values = noise
    return values.astype(jnp.bfloat16)


def draw_block_sides(key, part):
    device_count = BLOCKS // BLK_DEV
    keys = jax.random.split(key, device_count)
    perms = jax.vmap(lambda single: jax.random.permutation(single, BLK_DEV))(keys)
    return jnp.where(perms < BLK_DEV // 2, 1, 0).astype(jnp.int32).reshape(-1)


def setup_inputs(seed: int = 0) -> dict:
    key_list = jax.random.split(jax.random.key(seed), 4)
    vectors = draw_vectors(jax.random.fold_in(key_list[3], 71), 0)
    block_sides = draw_block_sides(jax.random.fold_in(key_list[3], 71), 0)
    centers = draw_centers(jax.random.fold_in(key_list[3], 71), 0)
    return {"vectors": vectors, "block_sides": block_sides, "centers": centers}


def refine_group(inputs):
    members, centroids = inputs
    member_count = members.shape[0]
    row_step = math.gcd(2048, member_count)
    score_scale = 4.0 / math.sqrt(D)
    stacked = members.reshape(member_count // row_step, row_step, D)
    for sweep_num in range(ITERS):
        sq_norms = lax.optimization_barrier(jnp.sum(centroids.astype(jnp.float32) ** 2, axis=1))

        def absorb(loop_state, row_block):
            numerator, denominator = loop_state
            scores = score_scale * (jnp.dot(row_block, centroids.T, preferred_element_type=jnp.float32) - 0.5 * sq_norms[None, :])
            weights = jax.nn.softmax(scores, axis=1).astype(jnp.bfloat16)
            numerator = numerator + jnp.dot(weights.T, row_block, preferred_element_type=jnp.float32)
            denominator = denominator + lax.optimization_barrier(jnp.sum(weights.astype(jnp.float32), axis=0))
            return ((numerator, denominator), None)
        initial = (jnp.zeros((K, D), jnp.float32), jnp.zeros((K,), jnp.float32))
        (numerator, denominator), unused = lax.scan(absorb, initial, stacked)
        centroids = ((numerator + centroids.astype(jnp.float32)) / (denominator + 1.0)[:, None]).astype(jnp.bfloat16)
    return centroids

def reference(vectors, block_sides, centers):
    per_device = VEC_DEV // BLK
    wide_idx = jnp.arange(N_WIDE, dtype=jnp.int32)
    low_bits = (wide_idx % 2 ** LEVEL)[:, None, None]
    labels = block_sides.reshape(N_WIDE, N_NARROW, per_device)
    group_ids = (low_bits + 2 ** LEVEL * labels).reshape(-1).astype(jnp.int32)
    block_order = jnp.argsort(group_ids, stable=True)
    grouped = jnp.take(vectors.reshape(-1, BLK, D), block_order, axis=0).reshape(GROUPS, -1, D)
    arranged = centers.reshape(LOOP, GROUPS, N_NARROW, KS, D).transpose(1, 2, 0, 3, 4).reshape(GROUPS, K, D)
    refined = lax.map(refine_group, (grouped, arranged))
    return refined.reshape(GROUPS, N_NARROW, LOOP, KS, D).transpose(2, 0, 1, 3, 4).reshape(GROUPS * K, D)
```

```python
import functools
import heapq
import math

import jax
import jax.numpy as jnp
from jax import lax
from jax.experimental import pallas as pl
from jax.experimental.pallas import tpu as pltpu
from jax.sharding import PartitionSpec as P

MESH = pl.DeviceIdType.MESH
D = 768
KS = 128
PIECE = 64
PIECES = 4
ROWS = PIECE * PIECES
SRC = 16
CHUNK = ROWS
ITERS = 2
Y_FIRST = (3,)
SCALE = 4.0 / math.sqrt(D) * math.log2(math.e)
F32 = jnp.float32
NT = (((1,), (1,)), ((), ()))


def hops(p, f, s):
    out = []
    if s == 0:
        relay = 1 if p % 2 == 0 else -1
        if f == 0:
            out += [("f", 1), ("f", -1)]
        elif (f == 1 and relay == 1) or (f == 3 and relay == -1):
            out.append(("f", relay))
        out += [("s", 1), ("s", -1)]
    else:
        relay = 1 if (p + f) % 2 == 0 else -1
        if (s == 1 and relay == 1) or (s == 3 and relay == -1):
            out.append(("s", relay))
    return out


def sends(key):
    p, dy, dz = key
    y_first = p in Y_FIRST
    f, s = (dy, dz) if y_first else (dz, dy)
    res = []
    for dim, step in hops(p, f, s):
        nf, ns = ((f + step) % 4, s) if dim == "f" else (f, (s + step) % 4)
        axis = ("y" if dim == "f" else "z") if y_first else ("z" if dim == "f" else "y")
        res.append((axis, step, (p, nf, ns) if y_first else (p, ns, nf)))
    return res


def plan():
    cost = {"y": 2.1, "z": 4.2}
    lat = {"y": 1.7, "z": 2.4}
    free = {}
    heap = [(0.0, 0, (0, 0, 0)), (0.0, 1, (1, 0, 0)), (5.0, 2, (2, 0, 0)), (7.0, 3, (3, 0, 0))]
    count = 4
    order = []
    while heap:
        now, unused, key = heapq.heappop(heap)
        order.append(key)
        for axis, step, target in sends(key):
            link = (axis, step)
            start = max(now, free.get(link, 0.0))
            free[link] = start + cost[axis]
            heapq.heappush(heap, (free[link] + lat[axis], count, target))
            count += 1
    return order, max(free.values())


def sem_of(key):
    p, dy, dz = key
    return p * 16 + dy * 4 + dz


def kernel(
    vec_ref, sides_ref, cen_ref, out_ref,
    x_all, swap_out, cen, hn, e_all, m_all, l_all, f_one, den_acc, lse_all, num, relay_in, main_in, den_out, den_in,
    x_send, x_recv, c_send, c_recv, l_send, l_recv, n_send, n_recv, d_send, d_recv,
):
    wide = lax.axis_index("wide")
    narrow = lax.axis_index("narrow")
    core = lax.rem(wide, 2)
    z = lax.rem(wide // 2, 8)
    y = lax.rem(narrow // 4, 2) * 2 + wide // 16
    x = lax.rem(narrow, 4)
    zp = z // 2
    parity = lax.rem(z, 2)
    me = y * 4 + zp

    def device(dx, ny, nz):
        nx = lax.rem(x + dx + 4, 4)
        return (lax.rem(ny, 2) * 16 + nz * 2 + core, (ny // 2) * 4 + nx)

    def plane(dy, dz):
        return device(0, lax.rem(y + dy + 4, 4), lax.rem(z + 2 * dz + 8, 8))

    def peer(index):
        return device(0, index // 4, lax.rem(index, 4) * 2 + parity)

    def across(dx):
        return device(dx, y, z)

    partner = device(0, y, z + 1 - 2 * parity)

    first = vec_ref[0:KS, :]
    second = vec_ref[KS : 2 * KS, :]
    first_stays = sides_ref[0] == parity
    base = pl.multiple_of(me * ROWS, ROWS)
    x_all[pl.ds(base, KS), :] = jnp.where(first_stays, first, second)
    swap_out[...] = jnp.where(first_stays, second, first)

    barrier = pltpu.get_barrier_semaphore()

    def greet(k, carry):
        pl.semaphore_signal(barrier, inc=1, device_id=peer(lax.rem(me + k, SRC)), device_id_type=MESH)
        return carry

    lax.fori_loop(1, SRC, greet, 0)
    for other in (partner, across(1), across(-1), across(2)):
        pl.semaphore_signal(barrier, inc=1, device_id=other, device_id_type=MESH)
    pl.semaphore_wait(barrier, SRC + 3)

    started = []

    def send(src, dst, send_sem, recv_sem, to):
        copy = pltpu.make_async_remote_copy(
            src_ref=src, dst_ref=dst, send_sem=send_sem, recv_sem=recv_sem, device_id=to, device_id_type=MESH
        )
        copy.start()
        started.append(copy)

    def arrived(dst, sem):
        pltpu.make_async_remote_copy(
            src_ref=dst, dst_ref=dst, send_sem=sem, recv_sem=sem, device_id=partner, device_id_type=MESH
        ).wait_recv()

    def piece(source, p):
        return x_all.at[pl.ds(pl.multiple_of(source * ROWS + p * PIECE, PIECE), PIECE), :]

    def source_of(dy, dz):
        return lax.rem(y - dy + 4, 4) * 4 + lax.rem(zp - dz + 4, 4)

    for half in (0, 1):
        send(
            swap_out.at[pl.ds(half * PIECE, PIECE), :], piece(me, 2 + half),
            x_send.at[sem_of((2 + half, 0, 0))], x_recv.at[sem_of((2 + half, 0, 0))], partner,
        )

    def send_centers(it, own):
        for step, slot in ((1, 1), (-1, 2)):
            for half in (0, 1) if step == 1 else (1, 0):
                rows = pl.ds(half * 64, 64)
                index = it * 6 + (slot - 1) * 2 + half
                send(
                    own.at[rows, :], cen.at[it, pl.ds(slot * KS + half * 64, 64), :],
                    c_send.at[index], c_recv.at[index], across(step),
                )

    def relay_centers(it):
        for step, slot, half in ((1, 1, 0), (-1, 2, 1)):
            rows = pl.ds(slot * KS + half * 64, 64)
            arrived(cen.at[it, rows, :], c_recv.at[it * 6 + (slot - 1) * 2 + half])
            index = it * 6 + 4 + half
            send(
                cen.at[it, rows, :], cen.at[it, pl.ds(3 * KS + half * 64, 64), :],
                c_send.at[index], c_recv.at[index], across(step),
            )

    def norms(it, q):
        c = cen[it, pl.ds(q * KS, KS), :].astype(F32)
        n = 0.5 * jnp.sum(c * c, axis=1, keepdims=True)
        hn[q] = jnp.broadcast_to(n, (KS, 128))

    def exponents(q, r, product):
        half = hn[q]
        s = (product - jnp.concatenate([half, half], axis=1)) * SCALE
        top = jnp.max(s, axis=0, keepdims=True)
        e = jnp.exp2(s - top)
        e_all[q, r] = e
        m_all[q, pl.ds(r, 1), :] = top
        l_all[q, pl.ds(r, 1), :] = jnp.sum(e, axis=0, keepdims=True)

    def scores(it, q, r):
        rows = x_all[pl.ds(pl.multiple_of(r * CHUNK, CHUNK), CHUNK), :]
        product = lax.dot_general(
            cen[it, pl.ds(q * KS, KS), :], rows, NT, preferred_element_type=F32
        )
        exponents(q, r, product)

    def score_chunk(r):
        rows = x_all[pl.ds(pl.multiple_of(r * CHUNK, CHUNK), CHUNK), :]
        for q in range(4):
            product = lax.dot_general(cen[0, pl.ds(q * KS, KS), :], rows, NT, preferred_element_type=F32)
            exponents(q, r, product)

    def score_block(it, q):
        norms(it, q)

        def one(r, carry):
            scores(it, q, r)
            return carry

        lax.fori_loop(0, SRC, one, 0)

    def exchange_lse(it):
        top = jnp.maximum(jnp.maximum(m_all[0], m_all[1]), jnp.maximum(m_all[2], m_all[3]))
        total = sum(l_all[q] * jnp.exp2(m_all[q] - top) for q in range(4))
        lse_all[it, me] = top + jnp.log2(total)

        def tell(k, carry):
            pltpu.make_async_remote_copy(
                src_ref=lse_all.at[it, me], dst_ref=lse_all.at[it, me],
                send_sem=l_send.at[it, k], recv_sem=l_recv.at[it, me],
                device_id=peer(lax.rem(me + k, SRC)), device_id_type=MESH,
            ).start()
            return carry

        lax.fori_loop(1, SRC, tell, 0)

        def hear(k, carry):
            other = lax.rem(me + k, SRC)
            arrived(lse_all.at[it, other], l_recv.at[it, other])
            return carry

        lax.fori_loop(1, SRC, hear, 0)
        best = lse_all[it, 0]
        for k in range(1, SRC):
            best = jnp.maximum(best, lse_all[it, k])
        total = jnp.exp2(lse_all[it, 0] - best)
        for k in range(1, SRC):
            total = total + jnp.exp2(lse_all[it, k] - best)
        return best + jnp.log2(total)

    def weigh(it, q, lse):
        f_one[q] = jnp.exp2(m_all[q] - lse)

        def group(g):
            parts = []
            den = jnp.zeros((KS, 128), F32)
            for j in range(4):
                r = g * 4 + j
                weights = (e_all[q, r] * f_one[q, pl.ds(r, 1), :]).astype(jnp.bfloat16)
                wide_weights = weights.astype(F32)
                den = den + wide_weights[:, :128] + wide_weights[:, 128:]
                parts.append(weights)
            rows = x_all[pl.ds(pl.multiple_of(g * 4 * CHUNK, 4 * CHUNK), 4 * CHUNK), :]
            term = jnp.dot(jnp.concatenate(parts, axis=1), rows, preferred_element_type=F32)
            return term, den

        num[it, q], den_acc[...] = group(0)

        def one(g, carry):
            term, den = group(g)
            num[it, q] += term
            den_acc[...] += den
            return carry

        lax.fori_loop(1, 4, one, 0)
        column = jnp.sum(den_acc[...], axis=1, keepdims=True)
        here = lax.broadcasted_iota(jnp.int32, (KS, 128), 0) == lax.broadcasted_iota(jnp.int32, (KS, 128), 1)
        row = jnp.sum(jnp.where(here, column, 0.0), axis=0, keepdims=True)
        den_out[it, q] = jnp.broadcast_to(row, (8, 128))

    def reduce_centers(it, lse, old):
        weigh(it, 3, lse)
        base = it * 6
        for i, (half, step) in enumerate(((0, 1), (1, -1))):
            send(
                num.at[it, 3, pl.ds(half * 64, 64), :], relay_in.at[it, i],
                n_send.at[base + i], n_recv.at[base + i], across(step),
            )
        send(den_out.at[it, 3], den_in.at[it, 3], d_send.at[it * 4 + 3], d_recv.at[it * 4 + 3], across(2))
        for i, (q, step, half) in enumerate(((2, 1, 1), (1, -1, 0))):
            weigh(it, q, lse)
            send(
                num.at[it, q, pl.ds(half * 64, 64), :], main_in.at[it, i, pl.ds(half * 64, 64), :],
                n_send.at[base + 2 + i], n_recv.at[base + 2 + i], across(step),
            )
            send(den_out.at[it, q], den_in.at[it, 3 - q], d_send.at[it * 4 + q], d_recv.at[it * 4 + 3 - q], across(step))
        for i, (q, step, half) in enumerate(((2, 1, 0), (1, -1, 1))):
            rows = pl.ds(half * 64, 64)
            arrived(relay_in.at[it, i], n_recv.at[base + i])
            num[it, q, rows, :] += relay_in[it, i]
            send(
                num.at[it, q, rows, :], main_in.at[it, i, rows, :],
                n_send.at[base + 4 + i], n_recv.at[base + 4 + i], across(step),
            )
        weigh(it, 0, lse)
        for i, half in enumerate((1, 0)):
            rows = pl.ds(half * 64, 64)
            arrived(main_in.at[it, i, rows, :], n_recv.at[base + 2 + i])
        for k in (1, 2, 3):
            arrived(den_in.at[it, k], d_recv.at[it * 4 + k])
        row = den_out[it, 0] + den_in[it, 1] + den_in[it, 2] + den_in[it, 3]
        here = lax.broadcasted_iota(jnp.int32, (KS, 128), 0) == lax.broadcasted_iota(jnp.int32, (KS, 128), 1)
        column = jnp.sum(jnp.where(here, row[0:1, :], 0.0), axis=1, keepdims=True)
        for i, half in enumerate((0, 1)):
            rows = pl.ds(half * 64, 64)
            arrived(main_in.at[it, i, rows, :], n_recv.at[base + 4 + i])
        total = num[it, 0] + main_in[it, 0] + main_in[it, 1]
        return ((total + old[...].astype(F32)) / (column + 1.0)).astype(jnp.bfloat16)

    order, unused = plan()
    seen = {}
    send_centers(0, cen_ref)
    cen[0, 0:KS, :] = cen_ref[...]
    norms(0, 0)
    ready = []
    centers_in = False
    for number, key in enumerate(order):
        p, dy, dz = key
        source = source_of(dy, dz)
        if key not in ((0, 0, 0), (1, 0, 0)):
            arrived(piece(source, p), x_recv.at[sem_of(key)])
        for axis, step, target in sends(key):
            to = plane(step, 0) if axis == "y" else plane(0, step)
            index = len([c for c in started if c is not None])
            send(piece(source, p), piece(source, p), x_send.at[64 + index - 6], x_recv.at[sem_of(target)], to)
        seen[(dy, dz)] = seen.get((dy, dz), 0) + 1
        if seen[(dy, dz)] == PIECES:
            ready.append(source)
        if number == 3:
            relay_centers(0)
        if number >= 12 and not centers_in:
            for index in (1, 2, 4, 5):
                slot, half = ((index // 2) + 1, index % 2) if index < 4 else (3, index - 4)
                arrived(cen.at[0, pl.ds(slot * KS + half * 64, 64), :], c_recv.at[index])
            for q in (1, 2, 3):
                norms(0, q)
            centers_in = True
        if centers_in:
            for r in ready:
                score_chunk(r)
            ready = []
    lse = exchange_lse(0)
    fresh = reduce_centers(0, lse, cen_ref)

    cen[1, 0:KS, :] = fresh
    own = cen.at[1, pl.ds(0, KS), :]
    send_centers(1, own)
    score_block(1, 0)
    relay_centers(1)
    for slot in (1, 2):
        half = 2 - slot
        arrived(cen.at[1, pl.ds(slot * KS + half * 64, 64), :], c_recv.at[6 + (slot - 1) * 2 + half])
        score_block(1, slot)
    for half in (0, 1):
        arrived(cen.at[1, pl.ds(3 * KS + half * 64, 64), :], c_recv.at[6 + 4 + half])
    score_block(1, 3)
    lse = exchange_lse(1)
    out_ref[...] = reduce_centers(1, lse, own)

    for copy in started:
        copy.wait_send()
    for it in range(ITERS):

        def told(k, carry):
            pltpu.make_async_remote_copy(
                src_ref=lse_all.at[it, me], dst_ref=lse_all.at[it, me],
                send_sem=l_send.at[it, k], recv_sem=l_recv.at[it, me], device_id=partner, device_id_type=MESH,
            ).wait_send()
            return carry

        lax.fori_loop(1, SRC, told, 0)


def local(vectors, block_sides, centers):
    vmem = pltpu.VMEM
    dma = pltpu.SemaphoreType.DMA
    whole = pl.BlockSpec(memory_space=pltpu.VMEM)
    return pl.pallas_call(
        kernel,
        out_shape=jax.ShapeDtypeStruct((KS, D), jnp.bfloat16),
        in_specs=[whole, pl.BlockSpec(memory_space=pltpu.SMEM), whole],
        out_specs=whole,
        scratch_shapes=[
            vmem((SRC * ROWS, D), jnp.bfloat16),
            vmem((KS, D), jnp.bfloat16),
            vmem((ITERS, 4 * KS, D), jnp.bfloat16),
            vmem((4, KS, 128), F32),
            vmem((4, SRC, KS, CHUNK), F32),
            vmem((4, SRC, CHUNK), F32),
            vmem((4, SRC, CHUNK), F32),
            vmem((4, SRC, CHUNK), F32),
            vmem((KS, 128), F32),
            vmem((ITERS, SRC, SRC, CHUNK), F32),
            vmem((ITERS, 4, KS, D), F32),
            vmem((ITERS, 2, 64, D), F32),
            vmem((ITERS, 2, KS, D), F32),
            vmem((ITERS, 4, 8, 128), F32),
            vmem((ITERS, 4, 8, 128), F32),
            dma((160,)), dma((64,)),
            dma((6 * ITERS,)), dma((6 * ITERS,)),
            dma((ITERS, SRC)), dma((ITERS, SRC)),
            dma((6 * ITERS,)), dma((6 * ITERS,)),
            dma((4 * ITERS,)), dma((4 * ITERS,)),
        ],
        compiler_params=pltpu.CompilerParams(
            collective_id=0, has_side_effects=True, vmem_limit_bytes=56 * 1024 * 1024
        ),
        name="refine",
    )(vectors, block_sides, centers)


def solution(mesh):
    in_specs = (P(("wide", "narrow"), None), P(("wide", "narrow")), P(("wide", "narrow"), None))
    out_specs = P(("wide", "narrow"), None)
    return jax.shard_map(local, mesh=mesh, in_specs=in_specs, out_specs=out_specs, check_vma=False)
```

```python
import functools
import heapq
import math

import jax
import jax.numpy as jnp
from jax import lax
from jax.experimental import pallas as pl
from jax.experimental.pallas import tpu as pltpu
from jax.sharding import PartitionSpec as P

MESH = pl.DeviceIdType.MESH
D = 768
KS = 128
PIECE = 64
PIECES = 4
ROWS = PIECE * PIECES
SRC = 16
CHUNK = ROWS
ITERS = 2
UNROLL = 2
SCALE = 4.0 / math.sqrt(D) * math.log2(math.e)
F32 = jnp.float32


def sends(key):
    p, dy, dz, dc = key
    out = []
    if dc == 1:
        return out
    if dy == 0 and dz == 0:
        out.append(("z+" if p % 2 == 0 else "z-", ("relay", p)))
    relay = 1 if (p + dz) % 2 == 0 else -1
    if dy == 0:
        out += [("y+", (p, 1, dz, 0)), ("y-", (p, 3, dz, 0))]
    elif (dy == 1 and relay == 1) or (dy == 3 and relay == -1):
        out.append(("y+" if relay == 1 else "y-", (p, 2, dz, 0)))
    out.append(("c", (p, dy, dz, 1)))
    return out


def plan():
    cost = {"y+": 2.1, "y-": 2.1, "z+": 4.2, "z-": 4.2, "c": 0.4}
    lat = {"y+": 1.7, "y-": 1.7, "z+": 2.4, "z-": 2.4, "c": 1.0}
    free = {}
    heap = [(0.0, 0, (0, 0, 0, 0)), (0.0, 1, (1, 0, 0, 0)), (6.0, 2, (2, 0, 0, 0)), (8.0, 3, (3, 0, 0, 0))]
    count = 4
    order = []
    while heap:
        now, unused, key = heapq.heappop(heap)
        order.append(key)
        if key[0] == "relay":
            out = [("z+" if key[1] % 2 == 0 else "z-", (key[1], 0, 1, 0))]
        else:
            out = sends(key)
        for link, target in out:
            start = max(now, free.get(link, 0.0))
            free[link] = start + cost[link]
            heapq.heappush(heap, (free[link] + lat[link], count, target))
            count += 1
    return order, max(free.values())


def sem_of(key):
    p, dy, dz, dc = key
    return p * 16 + dy * 4 + dz * 2 + dc


def kernel(
    vec_ref, sides_ref, cen_ref, out_ref,
    x_all, xt_all, swap_out, keep_out, relay_x, fin, cen, hn, e_all, m_all, l_all, f_one, den_acc, lse_all, num, relay_in, main_in, den_out, den_in,
    x_send, x_recv, r_send, r_recv, f_send, f_recv, c_send, c_recv, l_send, l_recv, n_send, n_recv, d_send, d_recv,
):
    wide = lax.axis_index("wide")
    narrow = lax.axis_index("narrow")
    core = lax.rem(wide, 2)
    z = lax.rem(wide // 2, 8)
    y = lax.rem(narrow // 4, 2) * 2 + wide // 16
    x = lax.rem(narrow, 4)
    zq = z // 4
    rest = lax.rem(z, 4)
    parity = lax.rem(z, 2)
    native = core == rest // 2
    foreign = core != rest // 2
    away = jnp.where(native, 0, 1)
    me = y * 4 + zq * 2 + core

    def device(dx, ny, nz, ncore):
        nx = lax.rem(x + dx + 4, 4)
        return (lax.rem(ny, 2) * 16 + nz * 2 + ncore, (ny // 2) * 4 + nx)

    def up(dy, dz, ncore):
        return device(0, lax.rem(y + dy + 4, 4), lax.rem(z + dz + 8, 8), ncore)

    def peer(index):
        return device(0, index // 4, lax.rem(index // 2, 2) * 4 + rest, lax.rem(index, 2))

    def across(dx):
        return device(dx, y, z, core)

    z_near = z + 1 - 2 * parity
    z_outer = lax.rem(z - 1 + 2 * parity + 8, 8)
    z_second = z + 2 - 4 * (rest // 2)
    near = device(0, y, z_near, 1 - core)
    outer = device(0, y, z_outer, 1 - core)
    second = device(0, y, z_second, core)
    mirror = device(0, y, z_second, 1 - core)

    first = vec_ref[0:KS, :]
    other_half = vec_ref[KS : 2 * KS, :]
    first_stays = sides_ref[0] == parity
    keep_out[...] = jnp.where(first_stays, first, other_half)
    swap_out[...] = jnp.where(first_stays, other_half, first)
    base = pl.multiple_of(me * ROWS, ROWS)

    @pl.when(native)
    def _():
        x_all[pl.ds(base, KS), :] = keep_out[...]
        cen[0, 0:KS, :] = cen_ref[...]

    barrier = pltpu.get_barrier_semaphore()

    def greet(k, carry):
        pl.semaphore_signal(barrier, inc=1, device_id=peer(lax.rem(me + k, SRC)), device_id_type=MESH)
        return carry

    lax.fori_loop(1, SRC, greet, 0)
    for other in (near, outer, mirror, up(0, 2, core), up(0, -2, core), across(1), across(-1), across(2)):
        pl.semaphore_signal(barrier, inc=1, device_id=other, device_id_type=MESH)
    pl.semaphore_wait(barrier, SRC - 1 + 8)

    started = []

    def send(src, dst, send_sem, recv_sem, to):
        copy = pltpu.make_async_remote_copy(
            src_ref=src, dst_ref=dst, send_sem=send_sem, recv_sem=recv_sem, device_id=to, device_id_type=MESH
        )
        copy.start()
        started.append(copy)

    def arrived(dst, sem):
        pltpu.make_async_remote_copy(
            src_ref=dst, dst_ref=dst, send_sem=sem, recv_sem=sem, device_id=near, device_id_type=MESH
        ).wait_recv()

    def piece(source, p):
        return x_all.at[pl.ds(pl.multiple_of(source * ROWS + p * PIECE, PIECE), PIECE), :]

    def source_of(dy, dz, dc):
        nz = zq if dz == 0 else 1 - zq
        return lax.rem(y - dy + 4, 4) * 4 + nz * 2 + (core if dc == 0 else 1 - core)

    to = tuple(jnp.where(native, a, b) for a, b in zip(near, outer))
    target = y * 4 + jnp.where(native, zq, z_outer // 4) * 2 + 1 - core
    for half in (0, 1):
        send(
            swap_out.at[pl.ds(half * PIECE, PIECE), :],
            x_all.at[pl.ds(pl.multiple_of(target * ROWS + away * KS + half * PIECE, PIECE), PIECE), :],
            x_send.at[half], x_recv.at[(2 * away + half) * 16], to,
        )

    def foreign_copies():
        yield pltpu.make_async_remote_copy(
            src_ref=cen_ref, dst_ref=cen.at[0, pl.ds(0, KS), :], send_sem=f_send.at[2], recv_sem=f_recv.at[0],
            device_id=mirror, device_id_type=MESH,
        )
        for half in (0, 1):
            yield pltpu.make_async_remote_copy(
                src_ref=keep_out.at[pl.ds(half * PIECE, PIECE), :], dst_ref=piece(me, 2 + half),
                send_sem=f_send.at[half], recv_sem=x_recv.at[(2 + half) * 16],
                device_id=second, device_id_type=MESH,
            )

    @pl.when(foreign)
    def _():
        for copy in foreign_copies():
            copy.start()

    def send_centers(it, own):
        for step, slot in ((1, 1), (-1, 2)):
            for half in (0, 1) if step == 1 else (1, 0):
                rows = pl.ds(half * 64, 64)
                index = it * 6 + (slot - 1) * 2 + half
                send(
                    own.at[rows, :], cen.at[it, pl.ds(slot * KS + half * 64, 64), :],
                    c_send.at[index], c_recv.at[index], across(step),
                )

    def relay_centers(it):
        for step, slot, half in ((1, 1, 0), (-1, 2, 1)):
            rows = pl.ds(slot * KS + half * 64, 64)
            arrived(cen.at[it, rows, :], c_recv.at[it * 6 + (slot - 1) * 2 + half])
            index = it * 6 + 4 + half
            send(
                cen.at[it, rows, :], cen.at[it, pl.ds(3 * KS + half * 64, 64), :],
                c_send.at[index], c_recv.at[index], across(step),
            )

    def norms(it, q):
        c = cen[it, pl.ds(q * KS, KS), :].astype(F32)
        n = 0.5 * jnp.sum(c * c, axis=1, keepdims=True)
        hn[q] = jnp.broadcast_to(n, (KS, 128))

    def exponents(q, r, product):
        half = hn[q]
        s = (product - jnp.concatenate([half, half], axis=1)) * SCALE
        top = jnp.max(s, axis=0, keepdims=True)
        e = jnp.exp2(s - top)
        e_all[q, r] = e
        m_all[q, pl.ds(r, 1), :] = top
        l_all[q, pl.ds(r, 1), :] = jnp.sum(e, axis=0, keepdims=True)

    def score_chunk(r):
        xt_all[r] = x_all[pl.ds(pl.multiple_of(r * CHUNK, CHUNK), CHUNK), :].T
        for q in range(4):
            exponents(q, r, jnp.dot(cen[0, pl.ds(q * KS, KS), :], xt_all[r], preferred_element_type=F32))

    def score_block(it, q, count=1):
        for k in range(count):
            norms(it, q + k)

        def one(g, carry):
            for j in range(UNROLL):
                r = g * UNROLL + j
                product = jnp.dot(
                    cen[it, pl.ds(q * KS, count * KS), :], xt_all[r], preferred_element_type=F32
                )
                for k in range(count):
                    exponents(q + k, r, product[k * KS : (k + 1) * KS, :])
            return carry

        lax.fori_loop(0, SRC // UNROLL, one, 0)

    def exchange_lse(it):
        top = jnp.maximum(jnp.maximum(m_all[0], m_all[1]), jnp.maximum(m_all[2], m_all[3]))
        total = sum(l_all[q] * jnp.exp2(m_all[q] - top) for q in range(4))
        lse_all[it, me] = top + jnp.log2(total)

        def tell(k, carry):
            pltpu.make_async_remote_copy(
                src_ref=lse_all.at[it, me], dst_ref=lse_all.at[it, me],
                send_sem=l_send.at[it, k], recv_sem=l_recv.at[it, me],
                device_id=peer(lax.rem(me + k, SRC)), device_id_type=MESH,
            ).start()
            return carry

        lax.fori_loop(1, SRC, tell, 0)

        def hear(k, carry):
            other = lax.rem(me + k, SRC)
            arrived(lse_all.at[it, other], l_recv.at[it, other])
            return carry

        lax.fori_loop(1, SRC, hear, 0)
        best = lse_all[it, 0]
        for k in range(1, SRC):
            best = jnp.maximum(best, lse_all[it, k])
        total = jnp.exp2(lse_all[it, 0] - best)
        for k in range(1, SRC):
            total = total + jnp.exp2(lse_all[it, k] - best)
        return best + jnp.log2(total)

    def weigh(it, q, lse):
        f_one[q] = jnp.exp2(m_all[q] - lse)

        def group(g):
            parts = []
            den = jnp.zeros((KS, 128), F32)
            for j in range(4):
                r = g * 4 + j
                weights = (e_all[q, r] * f_one[q, pl.ds(r, 1), :]).astype(jnp.bfloat16)
                wide_weights = weights.astype(F32)
                den = den + wide_weights[:, :128] + wide_weights[:, 128:]
                parts.append(weights)
            rows = x_all[pl.ds(pl.multiple_of(g * 4 * CHUNK, 4 * CHUNK), 4 * CHUNK), :]
            term = jnp.dot(jnp.concatenate(parts, axis=1), rows, preferred_element_type=F32)
            return term, den

        num[it, q], den_acc[...] = group(0)

        def one(g, carry):
            term, den = group(g)
            num[it, q] += term
            den_acc[...] += den
            return carry

        lax.fori_loop(1, 4, one, 0)
        column = jnp.sum(den_acc[...], axis=1, keepdims=True)
        here = lax.broadcasted_iota(jnp.int32, (KS, 128), 0) == lax.broadcasted_iota(jnp.int32, (KS, 128), 1)
        row = jnp.sum(jnp.where(here, column, 0.0), axis=0, keepdims=True)
        den_out[it, q] = jnp.broadcast_to(row, (8, 128))

    def reduce_centers(it, lse, old):
        weigh(it, 3, lse)
        base = it * 6
        for i, (half, step) in enumerate(((0, 1), (1, -1))):
            send(
                num.at[it, 3, pl.ds(half * 64, 64), :], relay_in.at[it, i],
                n_send.at[base + i], n_recv.at[base + i], across(step),
            )
        send(den_out.at[it, 3], den_in.at[it, 3], d_send.at[it * 4 + 3], d_recv.at[it * 4 + 3], across(2))
        for i, (q, step, half) in enumerate(((2, 1, 1), (1, -1, 0))):
            weigh(it, q, lse)
            send(
                num.at[it, q, pl.ds(half * 64, 64), :], main_in.at[it, i, pl.ds(half * 64, 64), :],
                n_send.at[base + 2 + i], n_recv.at[base + 2 + i], across(step),
            )
            send(den_out.at[it, q], den_in.at[it, 3 - q], d_send.at[it * 4 + q], d_recv.at[it * 4 + 3 - q], across(step))
        for i, (q, step, half) in enumerate(((2, 1, 0), (1, -1, 1))):
            rows = pl.ds(half * 64, 64)
            arrived(relay_in.at[it, i], n_recv.at[base + i])
            num[it, q, rows, :] += relay_in[it, i]
            send(
                num.at[it, q, rows, :], main_in.at[it, i, rows, :],
                n_send.at[base + 4 + i], n_recv.at[base + 4 + i], across(step),
            )
        weigh(it, 0, lse)
        for i, half in enumerate((1, 0)):
            rows = pl.ds(half * 64, 64)
            arrived(main_in.at[it, i, rows, :], n_recv.at[base + 2 + i])
        for k in (1, 2, 3):
            arrived(den_in.at[it, k], d_recv.at[it * 4 + k])
        row = den_out[it, 0] + den_in[it, 1] + den_in[it, 2] + den_in[it, 3]
        here = lax.broadcasted_iota(jnp.int32, (KS, 128), 0) == lax.broadcasted_iota(jnp.int32, (KS, 128), 1)
        column = jnp.sum(jnp.where(here, row[0:1, :], 0.0), axis=1, keepdims=True)
        for i, half in enumerate((0, 1)):
            rows = pl.ds(half * 64, 64)
            arrived(main_in.at[it, i, rows, :], n_recv.at[base + 4 + i])
        total = num[it, 0] + main_in[it, 0] + main_in[it, 1]
        return ((total + old[...].astype(F32)) / (column + 1.0)).astype(jnp.bfloat16)

    order, unused = plan()
    mine = cen.at[0, pl.ds(0, KS), :]
    seen = {}
    ready = []
    centers_in = False
    for number, key in enumerate(order):
        if key[0] == "relay":
            p = key[1]
            step = 2 if p % 2 == 0 else -2
            arrived(relay_x.at[p], r_recv.at[p])
            origin = y * 4 + lax.rem(z - step + 8, 8) // 4 * 2 + core
            send(relay_x.at[p], piece(origin, p), r_send.at[4 + p], x_recv.at[sem_of((p, 0, 1, 0))], up(0, step, core))
            continue
        p, dy, dz, dc = key
        source = source_of(dy, dz, dc)
        if key in ((0, 0, 0, 0), (1, 0, 0, 0)):

            @pl.when(foreign)
            def _():
                arrived(piece(source, p), x_recv.at[sem_of(key)])

        else:
            arrived(piece(source, p), x_recv.at[sem_of(key)])
        for link, goal in sends(key):
            if goal[0] == "relay":
                step = 2 if p % 2 == 0 else -2
                send(piece(source, p), relay_x.at[p], r_send.at[p], r_recv.at[p], up(0, step, core))
            else:
                to = up(0, 0, 1 - core) if link == "c" else up(1 if link == "y+" else -1, 0, core)
                send(piece(source, p), piece(source, p), x_send.at[len(started)], x_recv.at[sem_of(goal)], to)
        seen[(dy, dz, dc)] = seen.get((dy, dz, dc), 0) + 1
        if seen[(dy, dz, dc)] == PIECES:
            ready.append(source)
        if key == (1, 0, 0, 0):

            @pl.when(foreign)
            def _():
                arrived(mine, f_recv.at[0])

            send_centers(0, mine)
            norms(0, 0)
        if number == 8:
            relay_centers(0)
        if number >= 16 and not centers_in:
            for index in (1, 2, 4, 5):
                slot, half = ((index // 2) + 1, index % 2) if index < 4 else (3, index - 4)
                arrived(cen.at[0, pl.ds(slot * KS + half * 64, 64), :], c_recv.at[index])
            for q in (1, 2, 3):
                norms(0, q)
            centers_in = True
        if centers_in:
            for r in ready:
                score_chunk(r)
            ready = []
    lse = exchange_lse(0)
    fresh = reduce_centers(0, lse, mine)

    cen[1, 0:KS, :] = fresh
    own = cen.at[1, pl.ds(0, KS), :]
    send_centers(1, own)
    score_block(1, 0)
    relay_centers(1)
    for slot in (1, 2):
        half = 2 - slot
        arrived(cen.at[1, pl.ds(slot * KS + half * 64, 64), :], c_recv.at[6 + (slot - 1) * 2 + half])
    score_block(1, 1, 2)
    for half in (0, 1):
        arrived(cen.at[1, pl.ds(3 * KS + half * 64, 64), :], c_recv.at[6 + 4 + half])
    score_block(1, 3)
    lse = exchange_lse(1)
    fin[...] = reduce_centers(1, lse, own)

    @pl.when(native)
    def _():
        out_ref[...] = fin[...]

    @pl.when(foreign)
    def _():
        home = pltpu.make_async_remote_copy(
            src_ref=fin, dst_ref=out_ref, send_sem=f_send.at[3], recv_sem=f_recv.at[1],
            device_id=mirror, device_id_type=MESH,
        )
        home.start()
        home.wait()
        for copy in foreign_copies():
            copy.wait_send()

    for copy in started:
        copy.wait_send()
    for it in range(ITERS):

        def told(k, carry):
            pltpu.make_async_remote_copy(
                src_ref=lse_all.at[it, me], dst_ref=lse_all.at[it, me],
                send_sem=l_send.at[it, k], recv_sem=l_recv.at[it, me], device_id=near, device_id_type=MESH,
            ).wait_send()
            return carry

        lax.fori_loop(1, SRC, told, 0)


def local(vectors, block_sides, centers):
    vmem = pltpu.VMEM
    dma = pltpu.SemaphoreType.DMA
    whole = pl.BlockSpec(memory_space=pltpu.VMEM)
    return pl.pallas_call(
        kernel,
        out_shape=jax.ShapeDtypeStruct((KS, D), jnp.bfloat16),
        in_specs=[whole, pl.BlockSpec(memory_space=pltpu.SMEM), whole],
        out_specs=whole,
        scratch_shapes=[
            vmem((SRC * ROWS, D), jnp.bfloat16),
            vmem((SRC, D, CHUNK), jnp.bfloat16),
            vmem((KS, D), jnp.bfloat16),
            vmem((KS, D), jnp.bfloat16),
            vmem((PIECES, PIECE, D), jnp.bfloat16),
            vmem((KS, D), jnp.bfloat16),
            vmem((ITERS, 4 * KS, D), jnp.bfloat16),
            vmem((4, KS, 128), F32),
            vmem((4, SRC, KS, CHUNK), F32),
            vmem((4, SRC, CHUNK), F32),
            vmem((4, SRC, CHUNK), F32),
            vmem((4, SRC, CHUNK), F32),
            vmem((KS, 128), F32),
            vmem((ITERS, SRC, SRC, CHUNK), F32),
            vmem((ITERS, 4, KS, D), F32),
            vmem((ITERS, 2, 64, D), F32),
            vmem((ITERS, 2, KS, D), F32),
            vmem((ITERS, 4, 8, 128), F32),
            vmem((ITERS, 4, 8, 128), F32),
            dma((160,)), dma((64,)),
            dma((8,)), dma((4,)),
            dma((4,)), dma((2,)),
            dma((6 * ITERS,)), dma((6 * ITERS,)),
            dma((ITERS, SRC)), dma((ITERS, SRC)),
            dma((6 * ITERS,)), dma((6 * ITERS,)),
            dma((4 * ITERS,)), dma((4 * ITERS,)),
        ],
        compiler_params=pltpu.CompilerParams(
            collective_id=0, has_side_effects=True, vmem_limit_bytes=56 * 1024 * 1024
        ),
        name="refine",
    )(vectors, block_sides, centers)


def solution(mesh):
    in_specs = (P(("wide", "narrow"), None), P(("wide", "narrow")), P(("wide", "narrow"), None))
    out_specs = P(("wide", "narrow"), None)
    return jax.shard_map(local, mesh=mesh, in_specs=in_specs, out_specs=out_specs, check_vma=False)
```

```python
import functools
import heapq
import math

import jax
import jax.numpy as jnp
from jax import lax
from jax.experimental import pallas as pl
from jax.experimental.pallas import tpu as pltpu
from jax.sharding import PartitionSpec as P

MESH = pl.DeviceIdType.MESH
D = 768
KS = 128
PIECE = 64
PIECES = 4
ROWS = PIECE * PIECES
SRC = 16
CHUNK = ROWS
ITERS = 2
UNROLL = 2
LOW = (True, False)
AT = (22, 30, 38)
BF16 = jnp.bfloat16
SCALE = 4.0 / math.sqrt(D) * math.log2(math.e)
F32 = jnp.float32


def sends(key):
    p, dy, dz, dc = key
    out = []
    if dc == 1:
        return out
    if dy == 0 and dz == 0:
        out.append(("z+" if p % 2 == 0 else "z-", ("relay", p)))
    relay = 1 if (p + dz) % 2 == 0 else -1
    if dy == 0:
        out += [("y+", (p, 1, dz, 0)), ("y-", (p, 3, dz, 0))]
    elif (dy == 1 and relay == 1) or (dy == 3 and relay == -1):
        out.append(("y+" if relay == 1 else "y-", (p, 2, dz, 0)))
    out.append(("c", (p, dy, dz, 1)))
    return out


def plan():
    cost = {"y+": 2.1, "y-": 2.1, "z+": 4.2, "z-": 4.2, "c": 0.4}
    lat = {"y+": 1.7, "y-": 1.7, "z+": 2.4, "z-": 2.4, "c": 1.0}
    free = {}
    heap = [(0.0, 0, (0, 0, 0, 0)), (0.0, 1, (1, 0, 0, 0)), (6.0, 2, (2, 0, 0, 0)), (8.0, 3, (3, 0, 0, 0))]
    count = 4
    order = []
    while heap:
        now, unused, key = heapq.heappop(heap)
        order.append(key)
        if key[0] == "relay":
            out = [("z+" if key[1] % 2 == 0 else "z-", (key[1], 0, 1, 0))]
        else:
            out = sends(key)
        for link, target in out:
            start = max(now, free.get(link, 0.0))
            free[link] = start + cost[link]
            heapq.heappush(heap, (free[link] + lat[link], count, target))
            count += 1
    return order, max(free.values())


def sem_of(key):
    p, dy, dz, dc = key
    return p * 16 + dy * 4 + dz * 2 + dc


def kernel(
    vec_ref, sides_ref, cen_ref, out_ref,
    x_all, xt_all, swap_out, keep_out, relay_x, fin, cen, hn, e_all, m_all, l_all, f_one, den_acc, lse_two, lse_all, num, num_low,
    relay_f32, main_f32, relay_low, main_low, den_out, den_in,
    x_send, x_recv, go_sem, r_send, r_recv, f_send, f_recv, c_send, c_recv, l_send, l_recv, n_send, n_recv, d_send, d_recv,
):
    wide = lax.axis_index("wide")
    narrow = lax.axis_index("narrow")
    core = lax.rem(wide, 2)
    z = lax.rem(wide // 2, 8)
    y = lax.rem(narrow // 4, 2) * 2 + wide // 16
    x = lax.rem(narrow, 4)
    zq = z // 4
    rest = lax.rem(z, 4)
    parity = lax.rem(z, 2)
    native = core == rest // 2
    foreign = core != rest // 2
    away = jnp.where(native, 0, 1)
    me = y * 4 + zq * 2 + core

    def device(dx, ny, nz, ncore):
        nx = lax.rem(x + dx + 4, 4)
        return (lax.rem(ny, 2) * 16 + nz * 2 + ncore, (ny // 2) * 4 + nx)

    def up(dy, dz, ncore):
        return device(0, lax.rem(y + dy + 4, 4), lax.rem(z + dz + 8, 8), ncore)

    def peer(index):
        return device(0, index // 4, lax.rem(index // 2, 2) * 4 + rest, lax.rem(index, 2))

    def across(dx):
        return device(dx, y, z, core)

    z_near = z + 1 - 2 * parity
    z_outer = lax.rem(z - 1 + 2 * parity + 8, 8)
    z_second = z + 2 - 4 * (rest // 2)
    near = device(0, y, z_near, 1 - core)
    outer = device(0, y, z_outer, 1 - core)
    second = device(0, y, z_second, core)
    mirror = device(0, y, z_second, 1 - core)

    first = vec_ref[0:KS, :]
    other_half = vec_ref[KS : 2 * KS, :]
    first_stays = sides_ref[0] == parity
    keep_out[...] = jnp.where(first_stays, first, other_half)
    swap_out[...] = jnp.where(first_stays, other_half, first)
    base = pl.multiple_of(me * ROWS, ROWS)

    @pl.when(native)
    def _():
        x_all[pl.ds(base, KS), :] = keep_out[...]
        cen[0, 0:KS, :] = cen_ref[...]

    barrier = pltpu.get_barrier_semaphore()

    around = [up(dy, 0, core) for dy in (1, -1)] + [across(1), across(-1), up(0, 0, 1 - core)]
    around += [up(0, dz, c) for dz in (1, -1) for c in (core, 1 - core)]
    for other in around:
        pl.semaphore_signal(barrier, inc=1, device_id=other, device_id_type=MESH)
    pl.semaphore_wait(barrier, len(around))
    for dz in (1, -1):
        pl.semaphore_signal(go_sem, inc=1, device_id=up(0, dz, core), device_id_type=MESH)
    pl.semaphore_wait(go_sem, 2)

    started = []

    def send(src, dst, send_sem, recv_sem, to):
        copy = pltpu.make_async_remote_copy(
            src_ref=src, dst_ref=dst, send_sem=send_sem, recv_sem=recv_sem, device_id=to, device_id_type=MESH
        )
        copy.start()
        started.append(copy)

    def arrived(dst, sem):
        pltpu.make_async_remote_copy(
            src_ref=dst, dst_ref=dst, send_sem=sem, recv_sem=sem, device_id=near, device_id_type=MESH
        ).wait_recv()

    def piece(source, p):
        return x_all.at[pl.ds(pl.multiple_of(source * ROWS + p * PIECE, PIECE), PIECE), :]

    def source_of(dy, dz, dc):
        nz = zq if dz == 0 else 1 - zq
        return lax.rem(y - dy + 4, 4) * 4 + nz * 2 + (core if dc == 0 else 1 - core)

    to = tuple(jnp.where(native, a, b) for a, b in zip(near, outer))
    target = y * 4 + jnp.where(native, zq, z_outer // 4) * 2 + 1 - core
    for half in (0, 1):
        send(
            swap_out.at[pl.ds(half * PIECE, PIECE), :],
            x_all.at[pl.ds(pl.multiple_of(target * ROWS + away * KS + half * PIECE, PIECE), PIECE), :],
            x_send.at[half], x_recv.at[(2 * away + half) * 16], to,
        )

    def foreign_rows(half):
        return pltpu.make_async_remote_copy(
            src_ref=keep_out.at[pl.ds(half * PIECE, PIECE), :], dst_ref=piece(me, 2 + half),
            send_sem=f_send.at[half], recv_sem=x_recv.at[(2 + half) * 16], device_id=second, device_id_type=MESH,
        )

    def foreign_centers():
        return pltpu.make_async_remote_copy(
            src_ref=cen_ref, dst_ref=cen.at[0, pl.ds(0, KS), :], send_sem=f_send.at[2], recv_sem=f_recv.at[0],
            device_id=mirror, device_id_type=MESH,
        )

    @pl.when(foreign)
    def _():
        foreign_rows(0).start()
        foreign_rows(1).start()

    def send_centers(it, own):
        for step, slot in ((1, 1), (-1, 2)):
            for half in (0, 1) if step == 1 else (1, 0):
                rows = pl.ds(half * 64, 64)
                index = it * 6 + (slot - 1) * 2 + half
                send(
                    own.at[rows, :], cen.at[it, pl.ds(slot * KS + half * 64, 64), :],
                    c_send.at[index], c_recv.at[index], across(step),
                )

    def relay_centers(it):
        for step, slot, half in ((1, 1, 0), (-1, 2, 1)):
            rows = pl.ds(slot * KS + half * 64, 64)
            arrived(cen.at[it, rows, :], c_recv.at[it * 6 + (slot - 1) * 2 + half])
            index = it * 6 + 4 + half
            send(
                cen.at[it, rows, :], cen.at[it, pl.ds(3 * KS + half * 64, 64), :],
                c_send.at[index], c_recv.at[index], across(step),
            )

    def norms(it, q):
        c = cen[it, pl.ds(q * KS, KS), :].astype(F32)
        n = 0.5 * jnp.sum(c * c, axis=1, keepdims=True)
        hn[q] = jnp.broadcast_to(n, (KS, 128))

    def exponents(q, r, product):
        half = hn[q]
        s = (product - jnp.concatenate([half, half], axis=1)) * SCALE
        top = jnp.max(s, axis=0, keepdims=True)
        e = jnp.exp2(s - top)
        e_all[q, r] = e
        m_all[q, pl.ds(r, 1), :] = top
        l_all[q, pl.ds(r, 1), :] = jnp.sum(e, axis=0, keepdims=True)

    def score_chunk(r):
        xt_all[r] = x_all[pl.ds(pl.multiple_of(r * CHUNK, CHUNK), CHUNK), :].T
        for q in range(4):
            exponents(q, r, jnp.dot(cen[0, pl.ds(q * KS, KS), :], xt_all[r], preferred_element_type=F32))

    def score_block(it, q, count=1):
        for k in range(count):
            norms(it, q + k)

        def one(g, carry):
            for j in range(UNROLL):
                r = g * UNROLL + j
                product = jnp.dot(
                    cen[it, pl.ds(q * KS, count * KS), :], xt_all[r], preferred_element_type=F32
                )
                for k in range(count):
                    exponents(q + k, r, product[k * KS : (k + 1) * KS, :])
            return carry

        lax.fori_loop(0, SRC // UNROLL, one, 0)

    def log_add(parts):
        best = functools.reduce(jnp.maximum, parts)
        return best + jnp.log2(sum(jnp.exp2(part - best) for part in parts))

    def lse_copy(it, k):
        other = lax.rem(me // 2 + k, SRC // 2)
        return pltpu.make_async_remote_copy(
            src_ref=lse_all.at[it, me // 2], dst_ref=lse_all.at[it, me // 2],
            send_sem=l_send.at[it, k], recv_sem=l_recv.at[it, me // 2],
            device_id=peer(other * 2 + core), device_id_type=MESH,
        )

    def exchange_lse(it):
        top = jnp.maximum(jnp.maximum(m_all[0], m_all[1]), jnp.maximum(m_all[2], m_all[3]))
        total = sum(l_all[q] * jnp.exp2(m_all[q] - top) for q in range(4))
        lse_two[it, 0] = top + jnp.log2(total)
        send(lse_two.at[it, 0], lse_two.at[it, 1], l_send.at[it, 0], l_recv.at[it, SRC // 2], up(0, 0, 1 - core))
        arrived(lse_two.at[it, 1], l_recv.at[it, SRC // 2])
        lse_all[it, me // 2] = log_add([lse_two[it, 0], lse_two[it, 1]])

        def tell(k, carry):
            lse_copy(it, k).start()
            return carry

        lax.fori_loop(1, SRC // 2, tell, 0)

        def hear(k, carry):
            other = lax.rem(me // 2 + k, SRC // 2)
            arrived(lse_all.at[it, other], l_recv.at[it, other])
            return carry

        lax.fori_loop(1, SRC // 2, hear, 0)
        return log_add([lse_all[it, k] for k in range(SRC // 2)])

    def weigh(it, q, lse, count=1):
        blocks = range(count)
        for k in blocks:
            f_one[q + k] = jnp.exp2(m_all[q + k] - lse)

        def group(g, first):
            lines = []
            for k in blocks:
                parts = []
                den = jnp.zeros((KS, 128), F32)
                for j in range(4):
                    r = g * 4 + j
                    weights = (e_all[q + k, r] * f_one[q + k, pl.ds(r, 1), :]).astype(BF16)
                    wide_weights = weights.astype(F32)
                    den = den + wide_weights[:, :128] + wide_weights[:, 128:]
                    parts.append(weights)
                lines.append(jnp.concatenate(parts, axis=1))
                den_acc[q + k] = den if first else den_acc[q + k] + den
            rows = x_all[pl.ds(pl.multiple_of(g * 4 * CHUNK, 4 * CHUNK), 4 * CHUNK), :]
            weights = lines[0] if count == 1 else jnp.concatenate(lines, axis=0)
            term = jnp.dot(weights, rows, preferred_element_type=F32)
            for k in blocks:
                part = term[k * KS : (k + 1) * KS, :]
                num[it, q + k] = part if first else num[it, q + k] + part

        group(0, True)

        def one(g, carry):
            group(g, False)
            return carry

        lax.fori_loop(1, 4, one, 0)
        here = lax.broadcasted_iota(jnp.int32, (KS, 128), 0) == lax.broadcasted_iota(jnp.int32, (KS, 128), 1)
        for k in blocks:
            column = jnp.sum(den_acc[q + k], axis=1, keepdims=True)
            row = jnp.sum(jnp.where(here, column, 0.0), axis=0, keepdims=True)
            den_out[it, q + k] = jnp.broadcast_to(row, (8, 128))
            if LOW[it] and q + k > 0:
                num_low[it, q + k] = num[it, q + k].astype(BF16)

    def reduce_centers(it, lse, old):
        table, relay_in, main_in = (num_low, relay_low, main_low) if LOW[it] else (num, relay_f32, main_f32)
        weigh(it, 3, lse)
        base = it * 6
        for i, (half, step) in enumerate(((0, 1), (1, -1))):
            send(
                table.at[it, 3, pl.ds(half * 64, 64), :], relay_in.at[it, i],
                n_send.at[base + i], n_recv.at[base + i], across(step),
            )
        send(den_out.at[it, 3], den_in.at[it, 3], d_send.at[it * 4 + 3], d_recv.at[it * 4 + 3], across(2))
        weigh(it, 1, lse, 2)
        for i, (q, step, half) in enumerate(((2, 1, 1), (1, -1, 0))):
            send(
                table.at[it, q, pl.ds(half * 64, 64), :], main_in.at[it, i, pl.ds(half * 64, 64), :],
                n_send.at[base + 2 + i], n_recv.at[base + 2 + i], across(step),
            )
            send(den_out.at[it, q], den_in.at[it, 3 - q], d_send.at[it * 4 + q], d_recv.at[it * 4 + 3 - q], across(step))
        for i, (q, step, half) in enumerate(((2, 1, 0), (1, -1, 1))):
            rows = pl.ds(half * 64, 64)
            arrived(relay_in.at[it, i], n_recv.at[base + i])
            part = num[it, q, rows, :] + relay_in[it, i].astype(F32)
            table[it, q, rows, :] = part.astype(table.dtype)
            send(
                table.at[it, q, rows, :], main_in.at[it, i, rows, :],
                n_send.at[base + 4 + i], n_recv.at[base + 4 + i], across(step),
            )
        weigh(it, 0, lse)
        for i, half in enumerate((1, 0)):
            rows = pl.ds(half * 64, 64)
            arrived(main_in.at[it, i, rows, :], n_recv.at[base + 2 + i])
        for k in (1, 2, 3):
            arrived(den_in.at[it, k], d_recv.at[it * 4 + k])
        row = den_out[it, 0] + den_in[it, 1] + den_in[it, 2] + den_in[it, 3]
        here = lax.broadcasted_iota(jnp.int32, (KS, 128), 0) == lax.broadcasted_iota(jnp.int32, (KS, 128), 1)
        column = jnp.sum(jnp.where(here, row[0:1, :], 0.0), axis=1, keepdims=True)
        for i, half in enumerate((0, 1)):
            rows = pl.ds(half * 64, 64)
            arrived(main_in.at[it, i, rows, :], n_recv.at[base + 4 + i])
        total = num[it, 0] + main_in[it, 0].astype(F32) + main_in[it, 1].astype(F32)
        return ((total + old[...].astype(F32)) / (column + 1.0)).astype(BF16)

    order, unused = plan()
    mine = cen.at[0, pl.ds(0, KS), :]
    seen = {}
    ready = []
    phase = 0
    for number, key in enumerate(order):
        if key[0] == "relay":
            p = key[1]
            step = 2 if p % 2 == 0 else -2
            arrived(relay_x.at[p], r_recv.at[p])
            origin = y * 4 + lax.rem(z - step + 8, 8) // 4 * 2 + core
            send(relay_x.at[p], piece(origin, p), r_send.at[4 + p], x_recv.at[sem_of((p, 0, 1, 0))], up(0, step, core))
            continue
        p, dy, dz, dc = key
        source = source_of(dy, dz, dc)
        if key in ((0, 0, 0, 0), (1, 0, 0, 0)):

            @pl.when(foreign)
            def _():
                arrived(piece(source, p), x_recv.at[sem_of(key)])

        else:
            arrived(piece(source, p), x_recv.at[sem_of(key)])
        for link, goal in sends(key):
            if goal[0] == "relay":
                step = 2 if p % 2 == 0 else -2
                send(piece(source, p), relay_x.at[p], r_send.at[p], r_recv.at[p], up(0, step, core))
            else:
                to = up(0, 0, 1 - core) if link == "c" else up(1 if link == "y+" else -1, 0, core)
                send(piece(source, p), piece(source, p), x_send.at[len(started)], x_recv.at[sem_of(goal)], to)
        seen[(dy, dz, dc)] = seen.get((dy, dz, dc), 0) + 1
        if seen[(dy, dz, dc)] == PIECES:
            ready.append(source)
        if key == (3, 0, 0, 0):

            @pl.when(foreign)
            def _():
                foreign_centers().start()

        if number >= AT[0] and phase == 0:

            @pl.when(foreign)
            def _():
                arrived(mine, f_recv.at[0])

            send_centers(0, mine)
            norms(0, 0)
            phase = 1
        if number >= AT[1] and phase == 1:
            relay_centers(0)
            phase = 2
        if number >= AT[2] and phase == 2:
            for index in (1, 2, 4, 5):
                slot, half = ((index // 2) + 1, index % 2) if index < 4 else (3, index - 4)
                arrived(cen.at[0, pl.ds(slot * KS + half * 64, 64), :], c_recv.at[index])
            for q in (1, 2, 3):
                norms(0, q)
            phase = 3
        if phase == 3:
            if ready:
                score_chunk(ready.pop(0))
    for r in ready:
        score_chunk(r)
    lse = exchange_lse(0)
    fresh = reduce_centers(0, lse, mine)

    cen[1, 0:KS, :] = fresh
    own = cen.at[1, pl.ds(0, KS), :]
    send_centers(1, own)
    score_block(1, 0)
    relay_centers(1)
    for slot in (1, 2):
        half = 2 - slot
        arrived(cen.at[1, pl.ds(slot * KS + half * 64, 64), :], c_recv.at[6 + (slot - 1) * 2 + half])
    score_block(1, 1, 2)
    for half in (0, 1):
        arrived(cen.at[1, pl.ds(3 * KS + half * 64, 64), :], c_recv.at[6 + 4 + half])
    score_block(1, 3)
    lse = exchange_lse(1)
    fin[...] = reduce_centers(1, lse, own)

    @pl.when(native)
    def _():
        out_ref[...] = fin[...]

    @pl.when(foreign)
    def _():
        home = pltpu.make_async_remote_copy(
            src_ref=fin, dst_ref=out_ref, send_sem=f_send.at[3], recv_sem=f_recv.at[1],
            device_id=mirror, device_id_type=MESH,
        )
        home.start()
        home.wait()
        for copy in (foreign_rows(0), foreign_rows(1), foreign_centers()):
            copy.wait_send()

    for copy in started:
        copy.wait_send()
    for it in range(ITERS):

        def told(k, carry):
            lse_copy(it, k).wait_send()
            return carry

        lax.fori_loop(1, SRC // 2, told, 0)


def local(vectors, block_sides, centers):
    vmem = pltpu.VMEM
    dma = pltpu.SemaphoreType.DMA
    whole = pl.BlockSpec(memory_space=pltpu.VMEM)
    return pl.pallas_call(
        kernel,
        out_shape=jax.ShapeDtypeStruct((KS, D), jnp.bfloat16),
        in_specs=[whole, pl.BlockSpec(memory_space=pltpu.SMEM), whole],
        out_specs=whole,
        scratch_shapes=[
            vmem((SRC * ROWS, D), jnp.bfloat16),
            vmem((SRC, D, CHUNK), jnp.bfloat16),
            vmem((KS, D), jnp.bfloat16),
            vmem((KS, D), jnp.bfloat16),
            vmem((PIECES, PIECE, D), jnp.bfloat16),
            vmem((KS, D), jnp.bfloat16),
            vmem((ITERS, 4 * KS, D), jnp.bfloat16),
            vmem((4, KS, 128), F32),
            vmem((4, SRC, KS, CHUNK), F32),
            vmem((4, SRC, CHUNK), F32),
            vmem((4, SRC, CHUNK), F32),
            vmem((4, SRC, CHUNK), F32),
            vmem((4, KS, 128), F32),
            vmem((ITERS, 2, SRC, CHUNK), F32),
            vmem((ITERS, SRC // 2, SRC, CHUNK), F32),
            vmem((ITERS, 4, KS, D), F32),
            vmem((ITERS, 4, KS, D), BF16),
            vmem((ITERS, 2, 64, D), F32),
            vmem((ITERS, 2, KS, D), F32),
            vmem((ITERS, 2, 64, D), BF16),
            vmem((ITERS, 2, KS, D), BF16),
            vmem((ITERS, 4, 8, 128), F32),
            vmem((ITERS, 4, 8, 128), F32),
            dma((160,)), dma((64,)),
            pltpu.SemaphoreType.REGULAR,
            dma((8,)), dma((4,)),
            dma((4,)), dma((2,)),
            dma((6 * ITERS,)), dma((6 * ITERS,)),
            dma((ITERS, SRC)), dma((ITERS, SRC)),
            dma((6 * ITERS,)), dma((6 * ITERS,)),
            dma((4 * ITERS,)), dma((4 * ITERS,)),
        ],
        compiler_params=pltpu.CompilerParams(
            collective_id=0, has_side_effects=True, vmem_limit_bytes=56 * 1024 * 1024
        ),
        name="refine",
    )(vectors, block_sides, centers)


def solution(mesh):
    in_specs = (P(("wide", "narrow"), None), P(("wide", "narrow")), P(("wide", "narrow"), None))
    out_specs = P(("wide", "narrow"), None)
    return jax.shard_map(local, mesh=mesh, in_specs=in_specs, out_specs=out_specs, check_vma=False)
```

```python
import functools
import heapq
import math

import jax
import jax.numpy as jnp
from jax import lax
from jax.experimental import pallas as pl
from jax.experimental.pallas import tpu as pltpu
from jax.sharding import PartitionSpec as P

MESH = pl.DeviceIdType.MESH
D = 768
KS = 128
PIECE = 64
PIECES = 4
ROWS = PIECE * PIECES
SRC = 16
CHUNK = ROWS
ITERS = 2
UNROLL = 2
LOW = (True, False)
MIRROR = 17.0
MIRROR_AFTER = (1, 0, 0, 0)
COST = (2.1, 3.6, 0.4)
LATC = 4.0
START = (2.0, 4.0, 6.5, 8.5)
BF16 = jnp.bfloat16
SCALE = 4.0 / math.sqrt(D) * math.log2(math.e)
F32 = jnp.float32


def sends(key):
    p, dy, dz, dc = key
    out = []
    if dc == 1:
        return out
    if dy == 0 and dz == 0:
        out.append(("z+" if p % 2 == 0 else "z-", ("relay", p)))
    relay = 1 if (p + dz) % 2 == 0 else -1
    if dy == 0:
        out += [("y+", (p, 1, dz, 0)), ("y-", (p, 3, dz, 0))]
    elif (dy == 1 and relay == 1) or (dy == 3 and relay == -1):
        out.append(("y+" if relay == 1 else "y-", (p, 2, dz, 0)))
    out.append(("c", (p, dy, dz, 1)))
    return out


def plan():
    cost = {"y+": COST[0], "y-": COST[0], "z+": COST[1], "z-": COST[1], "c": COST[2], "x+": 2.1, "x-": 2.1}
    lat = {"y+": 1.7, "y-": 1.7, "z+": 2.4, "z-": 2.4, "c": LATC, "x+": 1.7, "x-": 1.7}
    free = {}
    heap = [(when, p, (p, 0, 0, 0)) for p, when in enumerate(START)]
    heap.append((MIRROR, 4, ("mirror",)))
    count = 5
    order = []
    while heap:
        now, unused, key = heapq.heappop(heap)
        order.append(key)
        if key[0] == "relay":
            out = [("z+" if key[1] % 2 == 0 else "z-", (key[1], 0, 1, 0))]
        elif key[0] == "mirror":
            out = [("x+", ("cen", 1, 0)), ("x-", ("cen", 2, 1)), ("x+", ("cen", 1, 1)), ("x-", ("cen", 2, 0))]
        elif key[0] == "cen":
            out = [("x+" if key[1] == 1 else "x-", ("cen", 3, key[2]))] if key[1:] in ((1, 0), (2, 1)) else []
        else:
            out = sends(key)
        for link, target in out:
            start = max(now, free.get(link, 0.0))
            free[link] = start + cost[link]
            heapq.heappush(heap, (free[link] + lat[link], count, target))
            count += 1
    return order, max(free.values())


def sem_of(key):
    p, dy, dz, dc = key
    return p * 16 + dy * 4 + dz * 2 + dc


def kernel(
    vec_ref, sides_ref, cen_ref, out_ref,
    x_all, xt_all, swap_out, keep_out, relay_x, fin, cen, hn, e_all, m_all, l_all, f_one, den_acc, lse_two, lse_all, num, num_low,
    relay_f32, main_f32, relay_low, main_low, den_out, den_in,
    x_send, x_recv, go_sem, r_send, r_recv, f_send, f_recv, c_send, c_recv, l_send, l_recv, n_send, n_recv, d_send, d_recv,
):
    wide = lax.axis_index("wide")
    narrow = lax.axis_index("narrow")
    core = lax.rem(wide, 2)
    z = lax.rem(wide // 2, 8)
    y = lax.rem(narrow // 4, 2) * 2 + wide // 16
    x = lax.rem(narrow, 4)
    zq = z // 4
    rest = lax.rem(z, 4)
    parity = lax.rem(z, 2)
    native = core == rest // 2
    foreign = core != rest // 2
    away = jnp.where(native, 0, 1)
    me = y * 4 + zq * 2 + core

    def device(dx, ny, nz, ncore):
        nx = lax.rem(x + dx + 4, 4)
        return (lax.rem(ny, 2) * 16 + nz * 2 + ncore, (ny // 2) * 4 + nx)

    def up(dy, dz, ncore):
        return device(0, lax.rem(y + dy + 4, 4), lax.rem(z + dz + 8, 8), ncore)

    def peer(index):
        return device(0, index // 4, lax.rem(index // 2, 2) * 4 + rest, lax.rem(index, 2))

    def across(dx):
        return device(dx, y, z, core)

    z_near = z + 1 - 2 * parity
    z_outer = lax.rem(z - 1 + 2 * parity + 8, 8)
    z_second = z + 2 - 4 * (rest // 2)
    near = device(0, y, z_near, 1 - core)
    outer = device(0, y, z_outer, 1 - core)
    second = device(0, y, z_second, core)
    mirror = device(0, y, z_second, 1 - core)

    first = vec_ref[0:KS, :]
    other_half = vec_ref[KS : 2 * KS, :]
    first_stays = sides_ref[0] == parity
    keep_out[...] = jnp.where(first_stays, first, other_half)
    swap_out[...] = jnp.where(first_stays, other_half, first)
    base = pl.multiple_of(me // 2 * (2 * ROWS) + core * KS, KS)

    @pl.when(native)
    def _():
        x_all[pl.ds(base, KS), :] = keep_out[...]
        cen[0, 0:KS, :] = cen_ref[...]

    barrier = pltpu.get_barrier_semaphore()

    around = [up(dy, 0, core) for dy in (1, -1)] + [across(1), across(-1), up(0, 0, 1 - core)]
    around += [up(0, dz, c) for dz in (1, -1) for c in (core, 1 - core)]
    for other in around:
        pl.semaphore_signal(barrier, inc=1, device_id=other, device_id_type=MESH)
    pl.semaphore_wait(barrier, len(around))
    for dz in (1, -1):
        pl.semaphore_signal(go_sem, inc=1, device_id=up(0, dz, core), device_id_type=MESH)
    pl.semaphore_wait(go_sem, 2)

    started = []

    def send(src, dst, send_sem, recv_sem, to):
        copy = pltpu.make_async_remote_copy(
            src_ref=src, dst_ref=dst, send_sem=send_sem, recv_sem=recv_sem, device_id=to, device_id_type=MESH
        )
        copy.start()
        started.append(copy)

    def arrived(dst, sem):
        pltpu.make_async_remote_copy(
            src_ref=dst, dst_ref=dst, send_sem=sem, recv_sem=sem, device_id=near, device_id_type=MESH
        ).wait_recv()

    def piece(source, p):
        start = source // 2 * (2 * ROWS) + p // 2 * ROWS + lax.rem(source, 2) * KS + p % 2 * PIECE
        return x_all.at[pl.ds(pl.multiple_of(start, PIECE), PIECE), :]

    def source_of(dy, dz, dc):
        nz = zq if dz == 0 else 1 - zq
        return lax.rem(y - dy + 4, 4) * 4 + nz * 2 + (core if dc == 0 else 1 - core)

    to = tuple(jnp.where(native, a, b) for a, b in zip(near, outer))
    target = (y * 2 + jnp.where(native, zq, z_outer // 4)) * (2 * ROWS) + (1 - core) * KS
    for half in (0, 1):
        send(
            swap_out.at[pl.ds(half * PIECE, PIECE), :],
            x_all.at[pl.ds(pl.multiple_of(target + away * ROWS + half * PIECE, PIECE), PIECE), :],
            x_send.at[half], x_recv.at[(2 * away + half) * 16], to,
        )

    def foreign_rows(half):
        return pltpu.make_async_remote_copy(
            src_ref=keep_out.at[pl.ds(half * PIECE, PIECE), :], dst_ref=piece(me, 2 + half),
            send_sem=f_send.at[half], recv_sem=x_recv.at[(2 + half) * 16], device_id=second, device_id_type=MESH,
        )

    def foreign_centers():
        return pltpu.make_async_remote_copy(
            src_ref=cen_ref, dst_ref=cen.at[0, pl.ds(0, KS), :], send_sem=f_send.at[2], recv_sem=f_recv.at[0],
            device_id=mirror, device_id_type=MESH,
        )

    @pl.when(foreign)
    def _():
        foreign_rows(0).start()
        foreign_rows(1).start()

    def send_centers(it, own):
        for step, slot in ((1, 1), (-1, 2)):
            for half in (0, 1) if step == 1 else (1, 0):
                rows = pl.ds(half * 64, 64)
                index = it * 6 + (slot - 1) * 2 + half
                send(
                    own.at[rows, :], cen.at[it, pl.ds(slot * KS + half * 64, 64), :],
                    c_send.at[index], c_recv.at[index], across(step),
                )

    def relay_center(it, slot, half):
        rows = pl.ds(slot * KS + half * 64, 64)
        arrived(cen.at[it, rows, :], c_recv.at[it * 6 + (slot - 1) * 2 + half])
        index = it * 6 + 4 + half
        send(
            cen.at[it, rows, :], cen.at[it, pl.ds(3 * KS + half * 64, 64), :],
            c_send.at[index], c_recv.at[index], across(1 if slot == 1 else -1),
        )

    def norms(it, q):
        c = cen[it, pl.ds(q * KS, KS), :].astype(F32)
        n = 0.5 * jnp.sum(c * c, axis=1, keepdims=True)
        hn[q] = jnp.broadcast_to(n, (KS, 128))

    def exponents(q, r, product):
        half = hn[q]
        s = (product - jnp.concatenate([half, half], axis=1)) * SCALE
        top = jnp.max(s, axis=0, keepdims=True)
        e = jnp.exp2(s - top)
        e_all[q, r] = e
        m_all[q, pl.ds(r, 1), :] = top
        l_all[q, pl.ds(r, 1), :] = jnp.sum(e, axis=0, keepdims=True)

    def score_chunk(r):
        xt_all[r] = x_all[pl.ds(pl.multiple_of(r * CHUNK, CHUNK), CHUNK), :].T
        for q in range(4):
            exponents(q, r, jnp.dot(cen[0, pl.ds(q * KS, KS), :], xt_all[r], preferred_element_type=F32))

    def score_block(it, q, count=1):
        for k in range(count):
            norms(it, q + k)

        def one(g, carry):
            for j in range(UNROLL):
                r = g * UNROLL + j
                product = jnp.dot(
                    cen[it, pl.ds(q * KS, count * KS), :], xt_all[r], preferred_element_type=F32
                )
                for k in range(count):
                    exponents(q + k, r, product[k * KS : (k + 1) * KS, :])
            return carry

        lax.fori_loop(0, SRC // UNROLL, one, 0)

    def log_add(parts):
        best = functools.reduce(jnp.maximum, parts)
        return best + jnp.log2(sum(jnp.exp2(part - best) for part in parts))

    def lse_copy(it, k):
        other = lax.rem(me // 2 + k, SRC // 2)
        return pltpu.make_async_remote_copy(
            src_ref=lse_all.at[it, me // 2], dst_ref=lse_all.at[it, me // 2],
            send_sem=l_send.at[it, k], recv_sem=l_recv.at[it, me // 2],
            device_id=peer(other * 2 + core), device_id_type=MESH,
        )

    def exchange_lse(it):
        top = jnp.maximum(jnp.maximum(m_all[0], m_all[1]), jnp.maximum(m_all[2], m_all[3]))
        total = sum(l_all[q] * jnp.exp2(m_all[q] - top) for q in range(4))
        lse_two[it, 0] = top + jnp.log2(total)
        send(lse_two.at[it, 0], lse_two.at[it, 1], l_send.at[it, 0], l_recv.at[it, SRC // 2], up(0, 0, 1 - core))
        arrived(lse_two.at[it, 1], l_recv.at[it, SRC // 2])
        lse_all[it, me // 2] = log_add([lse_two[it, 0], lse_two[it, 1]])

        def tell(k, carry):
            lse_copy(it, k).start()
            return carry

        lax.fori_loop(1, SRC // 2, tell, 0)

        def hear(k, carry):
            other = lax.rem(me // 2 + k, SRC // 2)
            arrived(lse_all.at[it, other], l_recv.at[it, other])
            return carry

        lax.fori_loop(1, SRC // 2, hear, 0)
        return log_add([lse_all[it, k] for k in range(SRC // 2)])

    def weigh(it, q, lse, count=1):
        blocks = range(count)
        for k in blocks:
            f_one[q + k] = jnp.exp2(m_all[q + k] - lse)

        def group(g, first):
            lines = []
            for k in blocks:
                parts = []
                den = jnp.zeros((KS, 128), F32)
                for j in range(4):
                    r = g * 4 + j
                    weights = (e_all[q + k, r] * f_one[q + k, pl.ds(r, 1), :]).astype(BF16)
                    wide_weights = weights.astype(F32)
                    den = den + wide_weights[:, :128] + wide_weights[:, 128:]
                    parts.append(weights)
                lines.append(jnp.concatenate(parts, axis=1))
                den_acc[q + k] = den if first else den_acc[q + k] + den
            rows = x_all[pl.ds(pl.multiple_of(g * 4 * CHUNK, 4 * CHUNK), 4 * CHUNK), :]
            weights = lines[0] if count == 1 else jnp.concatenate(lines, axis=0)
            term = jnp.dot(weights, rows, preferred_element_type=F32)
            for k in blocks:
                part = term[k * KS : (k + 1) * KS, :]
                num[it, q + k] = part if first else num[it, q + k] + part

        group(0, True)

        def one(g, carry):
            group(g, False)
            return carry

        lax.fori_loop(1, 4, one, 0)
        here = lax.broadcasted_iota(jnp.int32, (KS, 128), 0) == lax.broadcasted_iota(jnp.int32, (KS, 128), 1)
        for k in blocks:
            column = jnp.sum(den_acc[q + k], axis=1, keepdims=True)
            row = jnp.sum(jnp.where(here, column, 0.0), axis=0, keepdims=True)
            den_out[it, q + k] = jnp.broadcast_to(row, (8, 128))
            if LOW[it] and q + k > 0:
                num_low[it, q + k] = num[it, q + k].astype(BF16)

    def reduce_centers(it, lse, old):
        table, relay_in, main_in = (num_low, relay_low, main_low) if LOW[it] else (num, relay_f32, main_f32)
        weigh(it, 3, lse)
        base = it * 6
        for i, (half, step) in enumerate(((0, 1), (1, -1))):
            send(
                table.at[it, 3, pl.ds(half * 64, 64), :], relay_in.at[it, i],
                n_send.at[base + i], n_recv.at[base + i], across(step),
            )
        send(den_out.at[it, 3], den_in.at[it, 3], d_send.at[it * 4 + 3], d_recv.at[it * 4 + 3], across(2))
        weigh(it, 1, lse, 2)
        for i, (q, step, half) in enumerate(((2, 1, 1), (1, -1, 0))):
            send(
                table.at[it, q, pl.ds(half * 64, 64), :], main_in.at[it, i, pl.ds(half * 64, 64), :],
                n_send.at[base + 2 + i], n_recv.at[base + 2 + i], across(step),
            )
            send(den_out.at[it, q], den_in.at[it, 3 - q], d_send.at[it * 4 + q], d_recv.at[it * 4 + 3 - q], across(step))
        for i, (q, step, half) in enumerate(((2, 1, 0), (1, -1, 1))):
            rows = pl.ds(half * 64, 64)
            arrived(relay_in.at[it, i], n_recv.at[base + i])
            part = num[it, q, rows, :] + relay_in[it, i].astype(F32)
            table[it, q, rows, :] = part.astype(table.dtype)
            send(
                table.at[it, q, rows, :], main_in.at[it, i, rows, :],
                n_send.at[base + 4 + i], n_recv.at[base + 4 + i], across(step),
            )
        weigh(it, 0, lse)
        for i, half in enumerate((1, 0)):
            rows = pl.ds(half * 64, 64)
            arrived(main_in.at[it, i, rows, :], n_recv.at[base + 2 + i])
        for k in (1, 2, 3):
            arrived(den_in.at[it, k], d_recv.at[it * 4 + k])
        row = den_out[it, 0] + den_in[it, 1] + den_in[it, 2] + den_in[it, 3]
        here = lax.broadcasted_iota(jnp.int32, (KS, 128), 0) == lax.broadcasted_iota(jnp.int32, (KS, 128), 1)
        column = jnp.sum(jnp.where(here, row[0:1, :], 0.0), axis=1, keepdims=True)
        for i, half in enumerate((0, 1)):
            rows = pl.ds(half * 64, 64)
            arrived(main_in.at[it, i, rows, :], n_recv.at[base + 4 + i])
        total = num[it, 0] + main_in[it, 0].astype(F32) + main_in[it, 1].astype(F32)
        return ((total + old[...].astype(F32)) / (column + 1.0)).astype(BF16)

    order, unused = plan()
    mine = cen.at[0, pl.ds(0, KS), :]
    seen = {}
    ready = []
    blocks = 0
    for number, key in enumerate(order):
        if blocks == 7 and ready:
            score_chunk(ready.pop(0))
        if key[0] == "relay":
            p = key[1]
            step = 2 if p % 2 == 0 else -2
            arrived(relay_x.at[p], r_recv.at[p])
            origin = y * 4 + lax.rem(z - step + 8, 8) // 4 * 2 + core
            send(relay_x.at[p], piece(origin, p), r_send.at[4 + p], x_recv.at[sem_of((p, 0, 1, 0))], up(0, step, core))
            continue
        if key[0] == "mirror":

            @pl.when(foreign)
            def _():
                arrived(mine, f_recv.at[0])

            send_centers(0, mine)
            norms(0, 0)
            blocks += 1
            continue
        if key[0] == "cen":
            slot, half = key[1:]
            rows = pl.ds(slot * KS + half * 64, 64)
            if (slot, half) in ((1, 0), (2, 1)):
                relay_center(0, slot, half)
            else:
                arrived(cen.at[0, rows, :], c_recv.at[(slot - 1) * 2 + half])
            blocks += 1
            if blocks == 7:
                for q in (1, 2, 3):
                    norms(0, q)
            continue
        p, dy, dz, dc = key
        source = source_of(dy, dz, dc)
        if key in ((0, 0, 0, 0), (1, 0, 0, 0)):

            @pl.when(foreign)
            def _():
                arrived(piece(source, p), x_recv.at[sem_of(key)])

        else:
            arrived(piece(source, p), x_recv.at[sem_of(key)])
        for link, goal in sends(key):
            if goal[0] == "relay":
                step = 2 if p % 2 == 0 else -2
                send(piece(source, p), relay_x.at[p], r_send.at[p], r_recv.at[p], up(0, step, core))
            else:
                to = up(0, 0, 1 - core) if link == "c" else up(1 if link == "y+" else -1, 0, core)
                send(piece(source, p), piece(source, p), x_send.at[len(started)], x_recv.at[sem_of(goal)], to)
        if key == MIRROR_AFTER:

            @pl.when(foreign)
            def _():
                foreign_centers().start()

        chunk = (dy, dz, p // 2)
        seen[chunk] = seen.get(chunk, 0) + 1
        if seen[chunk] == PIECES:
            ready.append(source // 2 * 2 + p // 2)
    for r in ready:
        score_chunk(r)
    lse = exchange_lse(0)
    fresh = reduce_centers(0, lse, mine)

    cen[1, 0:KS, :] = fresh
    own = cen.at[1, pl.ds(0, KS), :]
    send_centers(1, own)
    score_block(1, 0)
    relay_center(1, 1, 0)
    relay_center(1, 2, 1)
    for slot in (1, 2):
        half = 2 - slot
        arrived(cen.at[1, pl.ds(slot * KS + half * 64, 64), :], c_recv.at[6 + (slot - 1) * 2 + half])
    score_block(1, 1, 2)
    for half in (0, 1):
        arrived(cen.at[1, pl.ds(3 * KS + half * 64, 64), :], c_recv.at[6 + 4 + half])
    score_block(1, 3)
    lse = exchange_lse(1)
    fin[...] = reduce_centers(1, lse, own)

    @pl.when(native)
    def _():
        out_ref[...] = fin[...]

    @pl.when(foreign)
    def _():
        home = pltpu.make_async_remote_copy(
            src_ref=fin, dst_ref=out_ref, send_sem=f_send.at[3], recv_sem=f_recv.at[1],
            device_id=mirror, device_id_type=MESH,
        )
        home.start()
        home.wait()
        for copy in (foreign_rows(0), foreign_rows(1), foreign_centers()):
            copy.wait_send()

    for copy in started:
        copy.wait_send()
    for it in range(ITERS):

        def told(k, carry):
            lse_copy(it, k).wait_send()
            return carry

        lax.fori_loop(1, SRC // 2, told, 0)


def local(vectors, block_sides, centers):
    vmem = pltpu.VMEM
    dma = pltpu.SemaphoreType.DMA
    whole = pl.BlockSpec(memory_space=pltpu.VMEM)
    return pl.pallas_call(
        kernel,
        out_shape=jax.ShapeDtypeStruct((KS, D), jnp.bfloat16),
        in_specs=[whole, pl.BlockSpec(memory_space=pltpu.SMEM), whole],
        out_specs=whole,
        scratch_shapes=[
            vmem((SRC * ROWS, D), jnp.bfloat16),
            vmem((SRC, D, CHUNK), jnp.bfloat16),
            vmem((KS, D), jnp.bfloat16),
            vmem((KS, D), jnp.bfloat16),
            vmem((PIECES, PIECE, D), jnp.bfloat16),
            vmem((KS, D), jnp.bfloat16),
            vmem((ITERS, 4 * KS, D), jnp.bfloat16),
            vmem((4, KS, 128), F32),
            vmem((4, SRC, KS, CHUNK), F32),
            vmem((4, SRC, CHUNK), F32),
            vmem((4, SRC, CHUNK), F32),
            vmem((4, SRC, CHUNK), F32),
            vmem((4, KS, 128), F32),
            vmem((ITERS, 2, SRC, CHUNK), F32),
            vmem((ITERS, SRC // 2, SRC, CHUNK), F32),
            vmem((ITERS, 4, KS, D), F32),
            vmem((ITERS, 4, KS, D), BF16),
            vmem((ITERS, 2, 64, D), F32),
            vmem((ITERS, 2, KS, D), F32),
            vmem((ITERS, 2, 64, D), BF16),
            vmem((ITERS, 2, KS, D), BF16),
            vmem((ITERS, 4, 8, 128), F32),
            vmem((ITERS, 4, 8, 128), F32),
            dma((160,)), dma((64,)),
            pltpu.SemaphoreType.REGULAR,
            dma((8,)), dma((4,)),
            dma((4,)), dma((2,)),
            dma((6 * ITERS,)), dma((6 * ITERS,)),
            dma((ITERS, SRC)), dma((ITERS, SRC)),
            dma((6 * ITERS,)), dma((6 * ITERS,)),
            dma((4 * ITERS,)), dma((4 * ITERS,)),
        ],
        compiler_params=pltpu.CompilerParams(
            collective_id=0, has_side_effects=True, vmem_limit_bytes=56 * 1024 * 1024
        ),
        name="refine",
    )(vectors, block_sides, centers)


def solution(mesh):
    in_specs = (P(("wide", "narrow"), None), P(("wide", "narrow")), P(("wide", "narrow"), None))
    out_specs = P(("wide", "narrow"), None)
    return jax.shard_map(local, mesh=mesh, in_specs=in_specs, out_specs=out_specs, check_vma=False)
```

```python
import functools
import heapq
import math

import jax
import jax.numpy as jnp
from jax import lax
from jax.experimental import pallas as pl
from jax.experimental.pallas import tpu as pltpu
from jax.sharding import PartitionSpec as P

MESH = pl.DeviceIdType.MESH
D = 768
KS = 128
PIECE = 64
PIECES = 4
ROWS = PIECE * PIECES
SRC = 16
CHUNK = ROWS
ITERS = 2
UNROLL = 2
LOW = (True, False)
MIRROR = 17.0
MIRROR_AFTER = (1, 0, 0, 0)
COST = (2.1, 3.6, 0.4)
LATC = 4.0
START = (2.0, 4.0, 6.5, 8.5)
BF16 = jnp.bfloat16
SCALE = 4.0 / math.sqrt(D) * math.log2(math.e)
F32 = jnp.float32


def sends(key):
    p, dy, dz, dc = key
    out = []
    if dc == 1:
        return out
    if dy == 0 and dz == 0:
        out.append(("z+" if p % 2 == 0 else "z-", ("relay", p)))
    relay = 1 if (p + dz) % 2 == 0 else -1
    if dy == 0:
        out += [("y+", (p, 1, dz, 0)), ("y-", (p, 3, dz, 0))]
    elif (dy == 1 and relay == 1) or (dy == 3 and relay == -1):
        out.append(("y+" if relay == 1 else "y-", (p, 2, dz, 0)))
    out.append(("c", (p, dy, dz, 1)))
    return out


def plan():
    cost = {"y+": COST[0], "y-": COST[0], "z+": COST[1], "z-": COST[1], "c": COST[2], "x+": 2.1, "x-": 2.1}
    lat = {"y+": 1.7, "y-": 1.7, "z+": 2.4, "z-": 2.4, "c": LATC, "x+": 1.7, "x-": 1.7}
    free = {}
    heap = [(when, p, (p, 0, 0, 0)) for p, when in enumerate(START)]
    heap.append((MIRROR, 4, ("mirror",)))
    count = 5
    order = []
    while heap:
        now, unused, key = heapq.heappop(heap)
        order.append(key)
        if key[0] == "relay":
            out = [("z+" if key[1] % 2 == 0 else "z-", (key[1], 0, 1, 0))]
        elif key[0] == "mirror":
            out = [("x+", ("cen", 1, 0)), ("x-", ("cen", 2, 1)), ("x+", ("cen", 1, 1)), ("x-", ("cen", 2, 0))]
        elif key[0] == "cen":
            out = [("x+" if key[1] == 1 else "x-", ("cen", 3, key[2]))] if key[1:] in ((1, 0), (2, 1)) else []
        else:
            out = sends(key)
        for link, target in out:
            start = max(now, free.get(link, 0.0))
            free[link] = start + cost[link]
            heapq.heappush(heap, (free[link] + lat[link], count, target))
            count += 1
    return order, max(free.values())


def sem_of(key):
    p, dy, dz, dc = key
    return p * 16 + dy * 4 + dz * 2 + dc


def kernel(
    vec_any, sides_ref, cen_any, out_ref,
    vec_ref, cen_ref,
    x_all, xt_all, swap_out, keep_out, relay_x, fin, cen, hn, e_all, m_all, l_all, f_one, den_acc, lse_two, lse_all, lse_sum, num, num_low,
    relay_f32, main_f32, relay_low, main_low, den_out, den_in,
    x_send, x_recv, go_sem, in_sem, r_send, r_recv, f_send, f_recv, c_send, c_recv, l_send, l_recv, n_send, n_recv, d_send, d_recv,
):
    wide = lax.axis_index("wide")
    narrow = lax.axis_index("narrow")
    core = lax.rem(wide, 2)
    z = lax.rem(wide // 2, 8)
    y = lax.rem(narrow // 4, 2) * 2 + wide // 16
    x = lax.rem(narrow, 4)
    zq = z // 4
    rest = lax.rem(z, 4)
    parity = lax.rem(z, 2)
    native = core == rest // 2
    foreign = core != rest // 2
    away = jnp.where(native, 0, 1)
    me = y * 4 + zq * 2 + core

    def device(dx, ny, nz, ncore):
        nx = lax.rem(x + dx + 4, 4)
        return (lax.rem(ny, 2) * 16 + nz * 2 + ncore, (ny // 2) * 4 + nx)

    def up(dy, dz, ncore):
        return device(0, lax.rem(y + dy + 4, 4), lax.rem(z + dz + 8, 8), ncore)

    def peer(index):
        return device(0, index // 4, lax.rem(index // 2, 2) * 4 + rest, lax.rem(index, 2))

    def across(dx):
        return device(dx, y, z, core)

    z_near = z + 1 - 2 * parity
    z_outer = lax.rem(z - 1 + 2 * parity + 8, 8)
    z_second = z + 2 - 4 * (rest // 2)
    near = device(0, y, z_near, 1 - core)
    outer = device(0, y, z_outer, 1 - core)
    second = device(0, y, z_second, core)
    mirror = device(0, y, z_second, 1 - core)

    vec_in = pltpu.make_async_copy(vec_any, vec_ref, in_sem.at[0])
    cen_in = pltpu.make_async_copy(cen_any, cen_ref, in_sem.at[1])
    vec_in.start()
    cen_in.start()
    barrier = pltpu.get_barrier_semaphore()

    around = [up(dy, 0, core) for dy in (1, -1)] + [across(1), across(-1), up(0, 0, 1 - core)]
    around += [up(0, dz, c) for dz in (1, -1) for c in (core, 1 - core)]
    for other in around:
        pl.semaphore_signal(barrier, inc=1, device_id=other, device_id_type=MESH)
    vec_in.wait()
    cen_in.wait()

    first = vec_ref[0:KS, :]
    other_half = vec_ref[KS : 2 * KS, :]
    first_stays = sides_ref[0] == parity
    keep_out[...] = jnp.where(first_stays, first, other_half)
    swap_out[...] = jnp.where(first_stays, other_half, first)
    base = pl.multiple_of(me // 2 * (2 * ROWS) + core * KS, KS)

    @pl.when(native)
    def _():
        x_all[pl.ds(base, KS), :] = keep_out[...]
        cen[0, 0:KS, :] = cen_ref[...]

    pl.semaphore_wait(barrier, len(around))
    for dz in (1, -1):
        pl.semaphore_signal(go_sem, inc=1, device_id=up(0, dz, core), device_id_type=MESH)
    pl.semaphore_wait(go_sem, 2)

    started = []

    def send(src, dst, send_sem, recv_sem, to):
        copy = pltpu.make_async_remote_copy(
            src_ref=src, dst_ref=dst, send_sem=send_sem, recv_sem=recv_sem, device_id=to, device_id_type=MESH
        )
        copy.start()
        started.append(copy)

    def arrived(dst, sem):
        pltpu.make_async_remote_copy(
            src_ref=dst, dst_ref=dst, send_sem=sem, recv_sem=sem, device_id=near, device_id_type=MESH
        ).wait_recv()

    def piece(source, p):
        start = source // 2 * (2 * ROWS) + p // 2 * ROWS + lax.rem(source, 2) * KS + p % 2 * PIECE
        return x_all.at[pl.ds(pl.multiple_of(start, PIECE), PIECE), :]

    def source_of(dy, dz, dc):
        nz = zq if dz == 0 else 1 - zq
        return lax.rem(y - dy + 4, 4) * 4 + nz * 2 + (core if dc == 0 else 1 - core)

    to = tuple(jnp.where(native, a, b) for a, b in zip(near, outer))
    target = (y * 2 + jnp.where(native, zq, z_outer // 4)) * (2 * ROWS) + (1 - core) * KS
    for half in (0, 1):
        send(
            swap_out.at[pl.ds(half * PIECE, PIECE), :],
            x_all.at[pl.ds(pl.multiple_of(target + away * ROWS + half * PIECE, PIECE), PIECE), :],
            x_send.at[half], x_recv.at[(2 * away + half) * 16], to,
        )

    def foreign_rows(half):
        return pltpu.make_async_remote_copy(
            src_ref=keep_out.at[pl.ds(half * PIECE, PIECE), :], dst_ref=piece(me, 2 + half),
            send_sem=f_send.at[half], recv_sem=x_recv.at[(2 + half) * 16], device_id=second, device_id_type=MESH,
        )

    def foreign_centers():
        return pltpu.make_async_remote_copy(
            src_ref=cen_ref, dst_ref=cen.at[0, pl.ds(0, KS), :], send_sem=f_send.at[2], recv_sem=f_recv.at[0],
            device_id=mirror, device_id_type=MESH,
        )

    @pl.when(foreign)
    def _():
        foreign_rows(0).start()
        foreign_rows(1).start()

    def send_centers(it, own):
        for step, slot in ((1, 1), (-1, 2)):
            for half in (0, 1) if step == 1 else (1, 0):
                rows = pl.ds(half * 64, 64)
                index = it * 6 + (slot - 1) * 2 + half
                send(
                    own.at[rows, :], cen.at[it, pl.ds(slot * KS + half * 64, 64), :],
                    c_send.at[index], c_recv.at[index], across(step),
                )

    def relay_center(it, slot, half):
        rows = pl.ds(slot * KS + half * 64, 64)
        arrived(cen.at[it, rows, :], c_recv.at[it * 6 + (slot - 1) * 2 + half])
        index = it * 6 + 4 + half
        send(
            cen.at[it, rows, :], cen.at[it, pl.ds(3 * KS + half * 64, 64), :],
            c_send.at[index], c_recv.at[index], across(1 if slot == 1 else -1),
        )

    def norms(it, q):
        c = cen[it, pl.ds(q * KS, KS), :].astype(F32)
        n = 0.5 * jnp.sum(c * c, axis=1, keepdims=True)
        hn[q] = jnp.broadcast_to(n, (KS, 128))

    def exponents(q, r, product):
        half = hn[q]
        s = (product - jnp.concatenate([half, half], axis=1)) * SCALE
        top = jnp.max(s, axis=0, keepdims=True)
        e = jnp.exp2(s - top)
        e_all[q, r] = e
        m_all[q, pl.ds(r, 1), :] = top
        l_all[q, pl.ds(r, 1), :] = jnp.sum(e, axis=0, keepdims=True)

    def score_chunk(r):
        xt_all[r] = x_all[pl.ds(pl.multiple_of(r * CHUNK, CHUNK), CHUNK), :].T
        for q in range(4):
            exponents(q, r, jnp.dot(cen[0, pl.ds(q * KS, KS), :], xt_all[r], preferred_element_type=F32))

    def score_rows(it, q, count, part):
        def one(g, carry):
            for j in range(UNROLL):
                r = g * UNROLL + j
                product = jnp.dot(
                    cen[it, pl.ds(q * KS, count * KS), :], xt_all[r], preferred_element_type=F32
                )
                for k in range(count):
                    exponents(q + k, r, product[k * KS : (k + 1) * KS, :])
            return carry

        groups = SRC // UNROLL
        first, last = (0, groups) if part is None else (part * groups // 2, (part + 1) * groups // 2)
        lax.fori_loop(first, last, one, 0)

    def score_block(it, q, count=1):
        for k in range(count):
            norms(it, q + k)
        score_rows(it, q, count, None)

    def log_add(parts):
        best = functools.reduce(jnp.maximum, parts)
        return best + jnp.log2(sum(jnp.exp2(part - best) for part in parts))

    def lines(part):
        return slice(0, SRC) if part is None else slice(part * 8, part * 8 + 8)

    def lse_copy(it, part, k):
        other = lax.rem(me // 2 + k, SRC // 2)
        there = lse_all.at[it, me // 2, lines(part), :]
        return pltpu.make_async_remote_copy(
            src_ref=there, dst_ref=there,
            send_sem=l_send.at[it, (part or 0) * 8 + k], recv_sem=l_recv.at[it, (part or 0) * 9 + me // 2],
            device_id=peer(other * 2 + core), device_id_type=MESH,
        )

    def lse_start(it, part):
        at = lines(part)
        tops = [m_all[q, at, :] for q in range(4)]
        top = functools.reduce(jnp.maximum, tops)
        total = sum(l_all[q, at, :] * jnp.exp2(tops[q] - top) for q in range(4))
        lse_two[it, 0, at, :] = top + jnp.log2(total)
        send(
            lse_two.at[it, 0, at, :], lse_two.at[it, 1, at, :],
            l_send.at[it, (part or 0) * 8], l_recv.at[it, (part or 0) * 9 + 8], up(0, 0, 1 - core),
        )

    def lse_tell(it, part):
        at = lines(part)
        arrived(lse_two.at[it, 1, at, :], l_recv.at[it, (part or 0) * 9 + 8])
        lse_all[it, me // 2, at, :] = log_add([lse_two[it, 0, at, :], lse_two[it, 1, at, :]])

        def tell(k, carry):
            lse_copy(it, part, k).start()
            return carry

        lax.fori_loop(1, SRC // 2, tell, 0)

    def lse_hear(it, part):
        at = lines(part)

        def hear(k, carry):
            other = lax.rem(me // 2 + k, SRC // 2)
            arrived(lse_all.at[it, other, at, :], l_recv.at[it, (part or 0) * 9 + other])
            return carry

        lax.fori_loop(1, SRC // 2, hear, 0)
        lse_sum[it, at, :] = log_add([lse_all[it, k, at, :] for k in range(SRC // 2)])

    def weigh(it, q, count=1, late=None):
        blocks = range(count)

        def factors(part):
            at = lines(part)
            for k in blocks:
                f_one[q + k, at, :] = jnp.exp2(m_all[q + k, at, :] - lse_sum[it, at, :])

        factors(None if late is None else 0)

        def group(g, first):
            rolls = []
            for k in blocks:
                parts = []
                den = jnp.zeros((KS, 128), F32)
                for j in range(4):
                    r = g * 4 + j
                    weights = (e_all[q + k, r] * f_one[q + k, pl.ds(r, 1), :]).astype(BF16)
                    wide_weights = weights.astype(F32)
                    den = den + wide_weights[:, :128] + wide_weights[:, 128:]
                    parts.append(weights)
                rolls.append(jnp.concatenate(parts, axis=1))
                den_acc[q + k] = den if first else den_acc[q + k] + den
            rows = x_all[pl.ds(pl.multiple_of(g * 4 * CHUNK, 4 * CHUNK), 4 * CHUNK), :]
            weights = rolls[0] if count == 1 else jnp.concatenate(rolls, axis=0)
            term = jnp.dot(weights, rows, preferred_element_type=F32)
            for k in blocks:
                part = term[k * KS : (k + 1) * KS, :]
                num[it, q + k] = part if first else num[it, q + k] + part

        group(0, True)

        def one(g, carry):
            group(g, False)
            return carry

        if late is None:
            lax.fori_loop(1, 4, one, 0)
        else:
            group(1, False)
            late()
            factors(1)
            lax.fori_loop(2, 4, one, 0)
        here = lax.broadcasted_iota(jnp.int32, (KS, 128), 0) == lax.broadcasted_iota(jnp.int32, (KS, 128), 1)
        for k in blocks:
            column = jnp.sum(den_acc[q + k], axis=1, keepdims=True)
            row = jnp.sum(jnp.where(here, column, 0.0), axis=0, keepdims=True)
            den_out[it, q + k] = jnp.broadcast_to(row, (8, 128))
            if LOW[it] and q + k > 0:
                num_low[it, q + k] = num[it, q + k].astype(BF16)

    def reduce_centers(it, old, late=None):
        table, relay_in, main_in = (num_low, relay_low, main_low) if LOW[it] else (num, relay_f32, main_f32)
        weigh(it, 3, late=late)
        base = it * 6
        for i, (half, step) in enumerate(((0, 1), (1, -1))):
            send(
                table.at[it, 3, pl.ds(half * 64, 64), :], relay_in.at[it, i],
                n_send.at[base + i], n_recv.at[base + i], across(step),
            )
        send(den_out.at[it, 3], den_in.at[it, 3], d_send.at[it * 4 + 3], d_recv.at[it * 4 + 3], across(2))
        weigh(it, 1, 2)
        for i, (q, step, half) in enumerate(((2, 1, 1), (1, -1, 0))):
            send(
                table.at[it, q, pl.ds(half * 64, 64), :], main_in.at[it, i, pl.ds(half * 64, 64), :],
                n_send.at[base + 2 + i], n_recv.at[base + 2 + i], across(step),
            )
            send(den_out.at[it, q], den_in.at[it, 3 - q], d_send.at[it * 4 + q], d_recv.at[it * 4 + 3 - q], across(step))
        for i, (q, step, half) in enumerate(((2, 1, 0), (1, -1, 1))):
            rows = pl.ds(half * 64, 64)
            arrived(relay_in.at[it, i], n_recv.at[base + i])
            part = num[it, q, rows, :] + relay_in[it, i].astype(F32)
            table[it, q, rows, :] = part.astype(table.dtype)
            send(
                table.at[it, q, rows, :], main_in.at[it, i, rows, :],
                n_send.at[base + 4 + i], n_recv.at[base + 4 + i], across(step),
            )
        weigh(it, 0)
        for i, half in enumerate((1, 0)):
            rows = pl.ds(half * 64, 64)
            arrived(main_in.at[it, i, rows, :], n_recv.at[base + 2 + i])
        for k in (1, 2, 3):
            arrived(den_in.at[it, k], d_recv.at[it * 4 + k])
        row = den_out[it, 0] + den_in[it, 1] + den_in[it, 2] + den_in[it, 3]
        here = lax.broadcasted_iota(jnp.int32, (KS, 128), 0) == lax.broadcasted_iota(jnp.int32, (KS, 128), 1)
        column = jnp.sum(jnp.where(here, row[0:1, :], 0.0), axis=1, keepdims=True)
        for i, half in enumerate((0, 1)):
            rows = pl.ds(half * 64, 64)
            arrived(main_in.at[it, i, rows, :], n_recv.at[base + 4 + i])
        total = num[it, 0] + main_in[it, 0].astype(F32) + main_in[it, 1].astype(F32)
        return ((total + old[...].astype(F32)) / (column + 1.0)).astype(BF16)

    order, unused = plan()
    mine = cen.at[0, pl.ds(0, KS), :]
    seen = {}
    ready = []
    blocks = 0
    for number, key in enumerate(order):
        if blocks == 7 and ready:
            score_chunk(ready.pop(0))
        if key[0] == "relay":
            p = key[1]
            step = 2 if p % 2 == 0 else -2
            arrived(relay_x.at[p], r_recv.at[p])
            origin = y * 4 + lax.rem(z - step + 8, 8) // 4 * 2 + core
            send(relay_x.at[p], piece(origin, p), r_send.at[4 + p], x_recv.at[sem_of((p, 0, 1, 0))], up(0, step, core))
            continue
        if key[0] == "mirror":

            @pl.when(foreign)
            def _():
                arrived(mine, f_recv.at[0])

            send_centers(0, mine)
            norms(0, 0)
            blocks += 1
            continue
        if key[0] == "cen":
            slot, half = key[1:]
            rows = pl.ds(slot * KS + half * 64, 64)
            if (slot, half) in ((1, 0), (2, 1)):
                relay_center(0, slot, half)
            else:
                arrived(cen.at[0, rows, :], c_recv.at[(slot - 1) * 2 + half])
            blocks += 1
            if blocks == 7:
                for q in (1, 2, 3):
                    norms(0, q)
            continue
        p, dy, dz, dc = key
        source = source_of(dy, dz, dc)
        if key in ((0, 0, 0, 0), (1, 0, 0, 0)):

            @pl.when(foreign)
            def _():
                arrived(piece(source, p), x_recv.at[sem_of(key)])

        else:
            arrived(piece(source, p), x_recv.at[sem_of(key)])
        for link, goal in sends(key):
            if goal[0] == "relay":
                step = 2 if p % 2 == 0 else -2
                send(piece(source, p), relay_x.at[p], r_send.at[p], r_recv.at[p], up(0, step, core))
            else:
                to = up(0, 0, 1 - core) if link == "c" else up(1 if link == "y+" else -1, 0, core)
                send(piece(source, p), piece(source, p), x_send.at[len(started)], x_recv.at[sem_of(goal)], to)
        if key == MIRROR_AFTER:

            @pl.when(foreign)
            def _():
                foreign_centers().start()

        chunk = (dy, dz, p // 2)
        seen[chunk] = seen.get(chunk, 0) + 1
        if seen[chunk] == PIECES:
            ready.append(source // 2 * 2 + p // 2)
    for r in ready:
        score_chunk(r)
    lse_start(0, None)
    lse_tell(0, None)
    lse_hear(0, None)
    fresh = reduce_centers(0, mine)

    cen[1, 0:KS, :] = fresh
    own = cen.at[1, pl.ds(0, KS), :]
    send_centers(1, own)
    score_block(1, 0)
    relay_center(1, 1, 0)
    relay_center(1, 2, 1)
    for slot in (1, 2):
        half = 2 - slot
        arrived(cen.at[1, pl.ds(slot * KS + half * 64, 64), :], c_recv.at[6 + (slot - 1) * 2 + half])
    score_block(1, 1, 2)
    for half in (0, 1):
        arrived(cen.at[1, pl.ds(3 * KS + half * 64, 64), :], c_recv.at[6 + 4 + half])
    norms(1, 3)
    score_rows(1, 3, 1, 0)
    lse_start(1, 0)
    score_rows(1, 3, 1, 1)
    lse_tell(1, 0)
    lse_start(1, 1)
    lse_tell(1, 1)
    lse_hear(1, 0)
    fin[...] = reduce_centers(1, own, lambda: lse_hear(1, 1))

    @pl.when(native)
    def _():
        out_ref[...] = fin[...]

    @pl.when(foreign)
    def _():
        home = pltpu.make_async_remote_copy(
            src_ref=fin, dst_ref=out_ref, send_sem=f_send.at[3], recv_sem=f_recv.at[1],
            device_id=mirror, device_id_type=MESH,
        )
        home.start()
        home.wait()
        for copy in (foreign_rows(0), foreign_rows(1), foreign_centers()):
            copy.wait_send()

    for copy in started:
        copy.wait_send()
    for it, part in ((0, None), (1, 0), (1, 1)):

        def told(k, carry):
            lse_copy(it, part, k).wait_send()
            return carry

        lax.fori_loop(1, SRC // 2, told, 0)


def local(vectors, block_sides, centers):
    vmem = pltpu.VMEM
    dma = pltpu.SemaphoreType.DMA
    whole = pl.BlockSpec(memory_space=pltpu.VMEM)
    return pl.pallas_call(
        kernel,
        out_shape=jax.ShapeDtypeStruct((KS, D), jnp.bfloat16),
        in_specs=[pl.BlockSpec(memory_space=pl.ANY), pl.BlockSpec(memory_space=pltpu.SMEM), pl.BlockSpec(memory_space=pl.ANY)],
        out_specs=whole,
        scratch_shapes=[
            vmem((2 * KS, D), jnp.bfloat16),
            vmem((KS, D), jnp.bfloat16),
            vmem((SRC * ROWS, D), jnp.bfloat16),
            vmem((SRC, D, CHUNK), jnp.bfloat16),
            vmem((KS, D), jnp.bfloat16),
            vmem((KS, D), jnp.bfloat16),
            vmem((PIECES, PIECE, D), jnp.bfloat16),
            vmem((KS, D), jnp.bfloat16),
            vmem((ITERS, 4 * KS, D), jnp.bfloat16),
            vmem((4, KS, 128), F32),
            vmem((4, SRC, KS, CHUNK), F32),
            vmem((4, SRC, CHUNK), F32),
            vmem((4, SRC, CHUNK), F32),
            vmem((4, SRC, CHUNK), F32),
            vmem((4, KS, 128), F32),
            vmem((ITERS, 2, SRC, CHUNK), F32),
            vmem((ITERS, SRC // 2, SRC, CHUNK), F32),
            vmem((ITERS, SRC, CHUNK), F32),
            vmem((ITERS, 4, KS, D), F32),
            vmem((ITERS, 4, KS, D), BF16),
            vmem((ITERS, 2, 64, D), F32),
            vmem((ITERS, 2, KS, D), F32),
            vmem((ITERS, 2, 64, D), BF16),
            vmem((ITERS, 2, KS, D), BF16),
            vmem((ITERS, 4, 8, 128), F32),
            vmem((ITERS, 4, 8, 128), F32),
            dma((160,)), dma((64,)),
            pltpu.SemaphoreType.REGULAR, dma((2,)),
            dma((8,)), dma((4,)),
            dma((4,)), dma((2,)),
            dma((6 * ITERS,)), dma((6 * ITERS,)),
            dma((ITERS, SRC)), dma((ITERS, 18)),
            dma((6 * ITERS,)), dma((6 * ITERS,)),
            dma((4 * ITERS,)), dma((4 * ITERS,)),
        ],
        compiler_params=pltpu.CompilerParams(
            collective_id=0, has_side_effects=True, vmem_limit_bytes=56 * 1024 * 1024
        ),
        name="refine",
    )(vectors, block_sides, centers)


def solution(mesh):
    in_specs = (P(("wide", "narrow"), None), P(("wide", "narrow")), P(("wide", "narrow"), None))
    out_specs = P(("wide", "narrow"), None)
    return jax.shard_map(local, mesh=mesh, in_specs=in_specs, out_specs=out_specs, check_vma=False)
```

```python
import functools
import heapq
import math

import jax
import jax.numpy as jnp
from jax import lax
from jax.experimental import pallas as pl
from jax.experimental.pallas import tpu as pltpu
from jax.sharding import PartitionSpec as P

MESH = pl.DeviceIdType.MESH
D = 768
KS = 128
PIECE = 64
PIECES = 4
ROWS = PIECE * PIECES
SRC = 16
CHUNK = ROWS
ITERS = 2
UNROLL = 2
LOW = (True, False)
MIRROR = 17.0
MIRROR_AFTER = (1, 0, 0, 0)
COST = (2.1, 3.6, 0.4)
LATC = 4.0
START = (2.0, 4.0, 6.5, 8.5)
BF16 = jnp.bfloat16
SCALE = 4.0 / math.sqrt(D) * math.log2(math.e)
F32 = jnp.float32


def sends(key):
    p, dy, dz, dc = key
    out = []
    if dc == 1:
        return out
    relay = 1 if (p + dz) % 2 == 0 else -1
    if dy == 0:
        out += [("y+", (p, 1, dz, 0)), ("y-", (p, 3, dz, 0))]
    elif (dy == 1 and relay == 1) or (dy == 3 and relay == -1):
        out.append(("y+" if relay == 1 else "y-", (p, 2, dz, 0)))
    if dy == 0 and dz == 0:
        out.append(("z+" if p % 2 == 0 else "z-", ("relay", p)))
    out.append(("c", (p, dy, dz, 1)))
    return out


def plan():
    cost = {"y+": COST[0], "y-": COST[0], "z+": COST[1], "z-": COST[1], "c": COST[2], "x+": 2.1, "x-": 2.1}
    lat = {"y+": 1.7, "y-": 1.7, "z+": 2.4, "z-": 2.4, "c": LATC, "x+": 1.7, "x-": 1.7}
    free = {}
    heap = [(when, p, (p, 0, 0, 0)) for p, when in enumerate(START)]
    heap.append((MIRROR, 4, ("mirror",)))
    count = 5
    order = []
    while heap:
        now, unused, key = heapq.heappop(heap)
        order.append(key)
        if key[0] == "relay":
            out = [("z+" if key[1] % 2 == 0 else "z-", (key[1], 0, 1, 0))]
        elif key[0] == "mirror":
            out = [("x+", ("cen", 1, 0)), ("x-", ("cen", 2, 1)), ("x+", ("cen", 1, 1)), ("x-", ("cen", 2, 0))]
        elif key[0] == "cen":
            out = [("x+" if key[1] == 1 else "x-", ("cen", 3, key[2]))] if key[1:] in ((1, 0), (2, 1)) else []
        else:
            out = sends(key)
        for link, target in out:
            start = max(now, free.get(link, 0.0))
            free[link] = start + cost[link]
            heapq.heappush(heap, (free[link] + lat[link], count, target))
            count += 1
    return order, max(free.values())


def sem_of(key):
    p, dy, dz, dc = key
    return p * 16 + dy * 4 + dz * 2 + dc


def kernel(
    vec_any, sides_ref, cen_any, out_ref,
    vec_ref, cen_ref,
    x_all, xt_all, swap_out, keep_out, relay_x, fin, cen, hn, e_all, m_all, l_all, f_one, den_acc, lse_two, lse_all, lse_sum, num, num_low,
    relay_f32, main_f32, relay_low, main_low, den_out, den_in,
    x_send, x_recv, go_sem, in_sem, r_send, r_recv, f_send, f_recv, c_send, c_recv, l_send, l_recv, n_send, n_recv, d_send, d_recv,
):
    wide = lax.axis_index("wide")
    narrow = lax.axis_index("narrow")
    core = lax.rem(wide, 2)
    z = lax.rem(wide // 2, 8)
    y = lax.rem(narrow // 4, 2) * 2 + wide // 16
    x = lax.rem(narrow, 4)
    zq = z // 4
    rest = lax.rem(z, 4)
    parity = lax.rem(z, 2)
    native = core == rest // 2
    foreign = core != rest // 2
    away = jnp.where(native, 0, 1)
    me = y * 4 + zq * 2 + core

    def device(dx, ny, nz, ncore):
        nx = lax.rem(x + dx + 4, 4)
        return (lax.rem(ny, 2) * 16 + nz * 2 + ncore, (ny // 2) * 4 + nx)

    def up(dy, dz, ncore):
        return device(0, lax.rem(y + dy + 4, 4), lax.rem(z + dz + 8, 8), ncore)

    def peer(index):
        return device(0, index // 4, lax.rem(index // 2, 2) * 4 + rest, lax.rem(index, 2))

    def across(dx):
        return device(dx, y, z, core)

    z_near = z + 1 - 2 * parity
    z_outer = lax.rem(z - 1 + 2 * parity + 8, 8)
    z_second = z + 2 - 4 * (rest // 2)
    near = device(0, y, z_near, 1 - core)
    outer = device(0, y, z_outer, 1 - core)
    second = device(0, y, z_second, core)
    mirror = device(0, y, z_second, 1 - core)

    vec_in = pltpu.make_async_copy(vec_any, vec_ref, in_sem.at[0])
    cen_in = pltpu.make_async_copy(cen_any, cen_ref, in_sem.at[1])
    vec_in.start()
    cen_in.start()
    barrier = pltpu.get_barrier_semaphore()

    around = [up(dy, 0, core) for dy in (1, -1)] + [across(1), across(-1), up(0, 0, 1 - core)]
    around += [up(0, dz, c) for dz in (1, -1) for c in (core, 1 - core)]
    for other in around:
        pl.semaphore_signal(barrier, inc=1, device_id=other, device_id_type=MESH)
    vec_in.wait()
    cen_in.wait()

    first = vec_ref[0:KS, :]
    other_half = vec_ref[KS : 2 * KS, :]
    first_stays = sides_ref[0] == parity
    keep_out[...] = jnp.where(first_stays, first, other_half)
    swap_out[...] = jnp.where(first_stays, other_half, first)
    base = pl.multiple_of(me // 2 * (2 * ROWS) + core * KS, KS)

    @pl.when(native)
    def _():
        x_all[pl.ds(base, KS), :] = keep_out[...]
        cen[0, 0:KS, :] = cen_ref[...]

    pl.semaphore_wait(barrier, len(around))
    for dz in (1, -1):
        pl.semaphore_signal(go_sem, inc=1, device_id=up(0, dz, core), device_id_type=MESH)

    started = []

    def send(src, dst, send_sem, recv_sem, to):
        copy = pltpu.make_async_remote_copy(
            src_ref=src, dst_ref=dst, send_sem=send_sem, recv_sem=recv_sem, device_id=to, device_id_type=MESH
        )
        copy.start()
        started.append(copy)

    def arrived(dst, sem):
        pltpu.make_async_remote_copy(
            src_ref=dst, dst_ref=dst, send_sem=sem, recv_sem=sem, device_id=near, device_id_type=MESH
        ).wait_recv()

    def piece(source, p):
        start = source // 2 * (2 * ROWS) + p // 2 * ROWS + lax.rem(source, 2) * KS + p % 2 * PIECE
        return x_all.at[pl.ds(pl.multiple_of(start, PIECE), PIECE), :]

    def source_of(dy, dz, dc):
        nz = zq if dz == 0 else 1 - zq
        return lax.rem(y - dy + 4, 4) * 4 + nz * 2 + (core if dc == 0 else 1 - core)

    to = tuple(jnp.where(native, a, b) for a, b in zip(near, outer))
    target = (y * 2 + jnp.where(native, zq, z_outer // 4)) * (2 * ROWS) + (1 - core) * KS
    for half in (0, 1):
        send(
            swap_out.at[pl.ds(half * PIECE, PIECE), :],
            x_all.at[pl.ds(pl.multiple_of(target + away * ROWS + half * PIECE, PIECE), PIECE), :],
            x_send.at[half], x_recv.at[(2 * away + half) * 16], to,
        )

    def foreign_rows(half):
        return pltpu.make_async_remote_copy(
            src_ref=keep_out.at[pl.ds(half * PIECE, PIECE), :], dst_ref=piece(me, 2 + half),
            send_sem=f_send.at[half], recv_sem=x_recv.at[(2 + half) * 16], device_id=second, device_id_type=MESH,
        )

    def foreign_centers():
        return pltpu.make_async_remote_copy(
            src_ref=cen_ref, dst_ref=cen.at[0, pl.ds(0, KS), :], send_sem=f_send.at[2], recv_sem=f_recv.at[0],
            device_id=mirror, device_id_type=MESH,
        )

    @pl.when(foreign)
    def _():
        pl.semaphore_wait(go_sem, 2)
        foreign_rows(0).start()
        foreign_rows(1).start()

    def send_centers(it, own):
        for step, slot in ((1, 1), (-1, 2)):
            for half in (0, 1) if step == 1 else (1, 0):
                rows = pl.ds(half * 64, 64)
                index = it * 6 + (slot - 1) * 2 + half
                send(
                    own.at[rows, :], cen.at[it, pl.ds(slot * KS + half * 64, 64), :],
                    c_send.at[index], c_recv.at[index], across(step),
                )

    def relay_center(it, slot, half):
        rows = pl.ds(slot * KS + half * 64, 64)
        arrived(cen.at[it, rows, :], c_recv.at[it * 6 + (slot - 1) * 2 + half])
        index = it * 6 + 4 + half
        send(
            cen.at[it, rows, :], cen.at[it, pl.ds(3 * KS + half * 64, 64), :],
            c_send.at[index], c_recv.at[index], across(1 if slot == 1 else -1),
        )

    def norms(it, q):
        c = cen[it, pl.ds(q * KS, KS), :].astype(F32)
        n = 0.5 * jnp.sum(c * c, axis=1, keepdims=True)
        hn[q] = jnp.broadcast_to(n, (KS, 128))

    def exponents(q, r, product):
        half = hn[q]
        s = (product - jnp.concatenate([half, half], axis=1)) * SCALE
        top = jnp.max(s, axis=0, keepdims=True)
        e = jnp.exp2(s - top)
        e_all[q, r] = e
        m_all[q, pl.ds(r, 1), :] = top
        l_all[q, pl.ds(r, 1), :] = jnp.sum(e, axis=0, keepdims=True)

    def score_chunk(r):
        xt_all[r] = x_all[pl.ds(pl.multiple_of(r * CHUNK, CHUNK), CHUNK), :].T
        for q in range(4):
            exponents(q, r, jnp.dot(cen[0, pl.ds(q * KS, KS), :], xt_all[r], preferred_element_type=F32))

    def score_rows(it, q, count, part):
        def one(g, carry):
            for j in range(UNROLL):
                r = g * UNROLL + j
                product = jnp.dot(
                    cen[it, pl.ds(q * KS, count * KS), :], xt_all[r], preferred_element_type=F32
                )
                for k in range(count):
                    exponents(q + k, r, product[k * KS : (k + 1) * KS, :])
            return carry

        groups = SRC // UNROLL
        first, last = (0, groups) if part is None else (part * groups // 2, (part + 1) * groups // 2)
        lax.fori_loop(first, last, one, 0)

    def score_block(it, q, count=1):
        for k in range(count):
            norms(it, q + k)
        score_rows(it, q, count, None)

    def log_add(parts):
        best = functools.reduce(jnp.maximum, parts)
        return best + jnp.log2(sum(jnp.exp2(part - best) for part in parts))

    def lines(part):
        return slice(0, SRC) if part is None else slice(part * 8, part * 8 + 8)

    def lse_copy(it, part, k):
        other = lax.rem(me // 2 + k, SRC // 2)
        there = lse_all.at[it, me // 2, lines(part), :]
        return pltpu.make_async_remote_copy(
            src_ref=there, dst_ref=there,
            send_sem=l_send.at[it, (part or 0) * 8 + k], recv_sem=l_recv.at[it, (part or 0) * 9 + me // 2],
            device_id=peer(other * 2 + core), device_id_type=MESH,
        )

    def lse_start(it, part):
        at = lines(part)
        tops = [m_all[q, at, :] for q in range(4)]
        top = functools.reduce(jnp.maximum, tops)
        total = sum(l_all[q, at, :] * jnp.exp2(tops[q] - top) for q in range(4))
        lse_two[it, 0, at, :] = top + jnp.log2(total)
        send(
            lse_two.at[it, 0, at, :], lse_two.at[it, 1, at, :],
            l_send.at[it, (part or 0) * 8], l_recv.at[it, (part or 0) * 9 + 8], up(0, 0, 1 - core),
        )

    def lse_tell(it, part):
        at = lines(part)
        arrived(lse_two.at[it, 1, at, :], l_recv.at[it, (part or 0) * 9 + 8])
        lse_all[it, me // 2, at, :] = log_add([lse_two[it, 0, at, :], lse_two[it, 1, at, :]])

        def tell(k, carry):
            lse_copy(it, part, k).start()
            return carry

        lax.fori_loop(1, SRC // 2, tell, 0)

    def lse_hear(it, part):
        at = lines(part)

        def hear(k, carry):
            other = lax.rem(me // 2 + k, SRC // 2)
            arrived(lse_all.at[it, other, at, :], l_recv.at[it, (part or 0) * 9 + other])
            return carry

        lax.fori_loop(1, SRC // 2, hear, 0)
        lse_sum[it, at, :] = log_add([lse_all[it, k, at, :] for k in range(SRC // 2)])

    def weigh(it, q, count=1, late=None):
        blocks = range(count)

        def factors(part):
            at = lines(part)
            for k in blocks:
                f_one[q + k, at, :] = jnp.exp2(m_all[q + k, at, :] - lse_sum[it, at, :])

        factors(None if late is None else 0)

        def group(g, first):
            rolls = []
            for k in blocks:
                parts = []
                den = jnp.zeros((KS, 128), F32)
                for j in range(4):
                    r = g * 4 + j
                    weights = (e_all[q + k, r] * f_one[q + k, pl.ds(r, 1), :]).astype(BF16)
                    wide_weights = weights.astype(F32)
                    den = den + wide_weights[:, :128] + wide_weights[:, 128:]
                    parts.append(weights)
                rolls.append(jnp.concatenate(parts, axis=1))
                den_acc[q + k] = den if first else den_acc[q + k] + den
            rows = x_all[pl.ds(pl.multiple_of(g * 4 * CHUNK, 4 * CHUNK), 4 * CHUNK), :]
            weights = rolls[0] if count == 1 else jnp.concatenate(rolls, axis=0)
            term = jnp.dot(weights, rows, preferred_element_type=F32)
            for k in blocks:
                part = term[k * KS : (k + 1) * KS, :]
                num[it, q + k] = part if first else num[it, q + k] + part

        group(0, True)

        def one(g, carry):
            group(g, False)
            return carry

        if late is None:
            lax.fori_loop(1, 4, one, 0)
        else:
            group(1, False)
            late()
            factors(1)
            lax.fori_loop(2, 4, one, 0)
        here = lax.broadcasted_iota(jnp.int32, (KS, 128), 0) == lax.broadcasted_iota(jnp.int32, (KS, 128), 1)
        for k in blocks:
            column = jnp.sum(den_acc[q + k], axis=1, keepdims=True)
            row = jnp.sum(jnp.where(here, column, 0.0), axis=0, keepdims=True)
            den_out[it, q + k] = jnp.broadcast_to(row, (8, 128))
            if LOW[it] and q + k > 0:
                num_low[it, q + k] = num[it, q + k].astype(BF16)

    def reduce_centers(it, old, late=None):
        table, relay_in, main_in = (num_low, relay_low, main_low) if LOW[it] else (num, relay_f32, main_f32)
        weigh(it, 3, late=late)
        base = it * 6
        for i, (half, step) in enumerate(((0, 1), (1, -1))):
            send(
                table.at[it, 3, pl.ds(half * 64, 64), :], relay_in.at[it, i],
                n_send.at[base + i], n_recv.at[base + i], across(step),
            )
        send(den_out.at[it, 3], den_in.at[it, 3], d_send.at[it * 4 + 3], d_recv.at[it * 4 + 3], across(2))
        weigh(it, 1, 2)
        for i, (q, step, half) in enumerate(((2, 1, 1), (1, -1, 0))):
            send(
                table.at[it, q, pl.ds(half * 64, 64), :], main_in.at[it, i, pl.ds(half * 64, 64), :],
                n_send.at[base + 2 + i], n_recv.at[base + 2 + i], across(step),
            )
            send(den_out.at[it, q], den_in.at[it, 3 - q], d_send.at[it * 4 + q], d_recv.at[it * 4 + 3 - q], across(step))
        for i, (q, step, half) in enumerate(((2, 1, 0), (1, -1, 1))):
            rows = pl.ds(half * 64, 64)
            arrived(relay_in.at[it, i], n_recv.at[base + i])
            part = num[it, q, rows, :] + relay_in[it, i].astype(F32)
            table[it, q, rows, :] = part.astype(table.dtype)
            send(
                table.at[it, q, rows, :], main_in.at[it, i, rows, :],
                n_send.at[base + 4 + i], n_recv.at[base + 4 + i], across(step),
            )
        weigh(it, 0)
        for i, half in enumerate((1, 0)):
            rows = pl.ds(half * 64, 64)
            arrived(main_in.at[it, i, rows, :], n_recv.at[base + 2 + i])
        for k in (1, 2, 3):
            arrived(den_in.at[it, k], d_recv.at[it * 4 + k])
        row = den_out[it, 0] + den_in[it, 1] + den_in[it, 2] + den_in[it, 3]
        here = lax.broadcasted_iota(jnp.int32, (KS, 128), 0) == lax.broadcasted_iota(jnp.int32, (KS, 128), 1)
        column = jnp.sum(jnp.where(here, row[0:1, :], 0.0), axis=1, keepdims=True)
        for i, half in enumerate((0, 1)):
            rows = pl.ds(half * 64, 64)
            arrived(main_in.at[it, i, rows, :], n_recv.at[base + 4 + i])
        total = num[it, 0] + main_in[it, 0].astype(F32) + main_in[it, 1].astype(F32)
        return ((total + old[...].astype(F32)) / (column + 1.0)).astype(BF16)

    order, unused = plan()
    mine = cen.at[0, pl.ds(0, KS), :]
    seen = {}
    ready = []
    blocks = 0
    for number, key in enumerate(order):
        if blocks == 7 and ready:
            score_chunk(ready.pop(0))
        if key[0] == "relay":
            p = key[1]
            step = 2 if p % 2 == 0 else -2
            arrived(relay_x.at[p], r_recv.at[p])
            origin = y * 4 + lax.rem(z - step + 8, 8) // 4 * 2 + core
            send(relay_x.at[p], piece(origin, p), r_send.at[4 + p], x_recv.at[sem_of((p, 0, 1, 0))], up(0, step, core))
            continue
        if key[0] == "mirror":

            @pl.when(foreign)
            def _():
                arrived(mine, f_recv.at[0])

            send_centers(0, mine)
            norms(0, 0)
            blocks += 1
            continue
        if key[0] == "cen":
            slot, half = key[1:]
            rows = pl.ds(slot * KS + half * 64, 64)
            if (slot, half) in ((1, 0), (2, 1)):
                relay_center(0, slot, half)
            else:
                arrived(cen.at[0, rows, :], c_recv.at[(slot - 1) * 2 + half])
            blocks += 1
            if blocks == 7:
                for q in (1, 2, 3):
                    norms(0, q)
            continue
        p, dy, dz, dc = key
        source = source_of(dy, dz, dc)
        if key in ((0, 0, 0, 0), (1, 0, 0, 0)):

            @pl.when(foreign)
            def _():
                arrived(piece(source, p), x_recv.at[sem_of(key)])

        else:
            arrived(piece(source, p), x_recv.at[sem_of(key)])
        for link, goal in sends(key):
            if goal[0] == "relay":
                if key == (0, 0, 0, 0):

                    @pl.when(native)
                    def _():
                        pl.semaphore_wait(go_sem, 2)

                step = 2 if p % 2 == 0 else -2
                send(piece(source, p), relay_x.at[p], r_send.at[p], r_recv.at[p], up(0, step, core))
            else:
                to = up(0, 0, 1 - core) if link == "c" else up(1 if link == "y+" else -1, 0, core)
                send(piece(source, p), piece(source, p), x_send.at[len(started)], x_recv.at[sem_of(goal)], to)
        if key == MIRROR_AFTER:

            @pl.when(foreign)
            def _():
                foreign_centers().start()

        chunk = (dy, dz, p // 2)
        seen[chunk] = seen.get(chunk, 0) + 1
        if seen[chunk] == PIECES:
            ready.append(source // 2 * 2 + p // 2)
    for r in ready:
        score_chunk(r)
    lse_start(0, None)
    lse_tell(0, None)
    lse_hear(0, None)
    fresh = reduce_centers(0, mine)

    cen[1, 0:KS, :] = fresh
    own = cen.at[1, pl.ds(0, KS), :]
    send_centers(1, own)
    score_block(1, 0)
    relay_center(1, 1, 0)
    relay_center(1, 2, 1)
    for slot in (1, 2):
        half = 2 - slot
        arrived(cen.at[1, pl.ds(slot * KS + half * 64, 64), :], c_recv.at[6 + (slot - 1) * 2 + half])
    score_block(1, 1, 2)
    for half in (0, 1):
        arrived(cen.at[1, pl.ds(3 * KS + half * 64, 64), :], c_recv.at[6 + 4 + half])
    norms(1, 3)
    score_rows(1, 3, 1, 0)
    lse_start(1, 0)
    score_rows(1, 3, 1, 1)
    lse_tell(1, 0)
    lse_start(1, 1)
    lse_tell(1, 1)
    lse_hear(1, 0)
    fin[...] = reduce_centers(1, own, lambda: lse_hear(1, 1))

    @pl.when(native)
    def _():
        out_ref[...] = fin[...]

    @pl.when(foreign)
    def _():
        home = pltpu.make_async_remote_copy(
            src_ref=fin, dst_ref=out_ref, send_sem=f_send.at[3], recv_sem=f_recv.at[1],
            device_id=mirror, device_id_type=MESH,
        )
        home.start()
        home.wait()
        for copy in (foreign_rows(0), foreign_rows(1), foreign_centers()):
            copy.wait_send()

    for copy in started:
        copy.wait_send()
    for it, part in ((0, None), (1, 0), (1, 1)):

        def told(k, carry):
            lse_copy(it, part, k).wait_send()
            return carry

        lax.fori_loop(1, SRC // 2, told, 0)


def local(vectors, block_sides, centers):
    vmem = pltpu.VMEM
    dma = pltpu.SemaphoreType.DMA
    whole = pl.BlockSpec(memory_space=pltpu.VMEM)
    return pl.pallas_call(
        kernel,
        out_shape=jax.ShapeDtypeStruct((KS, D), jnp.bfloat16),
        in_specs=[pl.BlockSpec(memory_space=pl.ANY), pl.BlockSpec(memory_space=pltpu.SMEM), pl.BlockSpec(memory_space=pl.ANY)],
        out_specs=whole,
        scratch_shapes=[
            vmem((2 * KS, D), jnp.bfloat16),
            vmem((KS, D), jnp.bfloat16),
            vmem((SRC * ROWS, D), jnp.bfloat16),
            vmem((SRC, D, CHUNK), jnp.bfloat16),
            vmem((KS, D), jnp.bfloat16),
            vmem((KS, D), jnp.bfloat16),
            vmem((PIECES, PIECE, D), jnp.bfloat16),
            vmem((KS, D), jnp.bfloat16),
            vmem((ITERS, 4 * KS, D), jnp.bfloat16),
            vmem((4, KS, 128), F32),
            vmem((4, SRC, KS, CHUNK), F32),
            vmem((4, SRC, CHUNK), F32),
            vmem((4, SRC, CHUNK), F32),
            vmem((4, SRC, CHUNK), F32),
            vmem((4, KS, 128), F32),
            vmem((ITERS, 2, SRC, CHUNK), F32),
            vmem((ITERS, SRC // 2, SRC, CHUNK), F32),
            vmem((ITERS, SRC, CHUNK), F32),
            vmem((ITERS, 4, KS, D), F32),
            vmem((ITERS, 4, KS, D), BF16),
            vmem((ITERS, 2, 64, D), F32),
            vmem((ITERS, 2, KS, D), F32),
            vmem((ITERS, 2, 64, D), BF16),
            vmem((ITERS, 2, KS, D), BF16),
            vmem((ITERS, 4, 8, 128), F32),
            vmem((ITERS, 4, 8, 128), F32),
            dma((160,)), dma((64,)),
            pltpu.SemaphoreType.REGULAR, dma((2,)),
            dma((8,)), dma((4,)),
            dma((4,)), dma((2,)),
            dma((6 * ITERS,)), dma((6 * ITERS,)),
            dma((ITERS, SRC)), dma((ITERS, 18)),
            dma((6 * ITERS,)), dma((6 * ITERS,)),
            dma((4 * ITERS,)), dma((4 * ITERS,)),
        ],
        compiler_params=pltpu.CompilerParams(
            collective_id=0, has_side_effects=True, vmem_limit_bytes=56 * 1024 * 1024
        ),
        name="refine",
    )(vectors, block_sides, centers)


def solution(mesh):
    in_specs = (P(("wide", "narrow"), None), P(("wide", "narrow")), P(("wide", "narrow"), None))
    out_specs = P(("wide", "narrow"), None)
    return jax.shard_map(local, mesh=mesh, in_specs=in_specs, out_specs=out_specs, check_vma=False)
```

```python
import functools
import heapq
import math

import jax
import jax.numpy as jnp
from jax import lax
from jax.experimental import pallas as pl
from jax.experimental.pallas import tpu as pltpu
from jax.sharding import PartitionSpec as P

MESH = pl.DeviceIdType.MESH
D = 768
KS = 128
PIECE = 64
PIECES = 4
ROWS = PIECE * PIECES
SRC = 16
CHUNK = ROWS
ITERS = 2
UNROLL = 2
LOW = (True, False)
MIRROR = 17.0
MIRROR_AFTER = (1, 0, 0, 0)
COST = (2.1, 3.6, 0.4)
LATC = 4.0
START = (2.0, 4.0, 6.5, 8.5)
BF16 = jnp.bfloat16
SCALE = 4.0 / math.sqrt(D) * math.log2(math.e)
F32 = jnp.float32


def sends(key):
    p, dy, dz, dc = key
    out = []
    if dc == 1:
        return out
    if dy == 0 and dz == 0:
        out.append(("z+" if p % 2 == 0 else "z-", ("relay", p)))
    relay = 1 if (p + dz) % 2 == 0 else -1
    if dy == 0:
        out += [("y+", (p, 1, dz, 0)), ("y-", (p, 3, dz, 0))]
    elif (dy == 1 and relay == 1) or (dy == 3 and relay == -1):
        out.append(("y+" if relay == 1 else "y-", (p, 2, dz, 0)))
    out.append(("c", (p, dy, dz, 1)))
    return out


def plan():
    cost = {"y+": COST[0], "y-": COST[0], "z+": COST[1], "z-": COST[1], "c": COST[2], "x+": 2.1, "x-": 2.1}
    lat = {"y+": 1.7, "y-": 1.7, "z+": 2.4, "z-": 2.4, "c": LATC, "x+": 1.7, "x-": 1.7}
    free = {}
    heap = [(when, p, (p, 0, 0, 0)) for p, when in enumerate(START)]
    heap.append((MIRROR, 4, ("mirror",)))
    count = 5
    order = []
    while heap:
        now, unused, key = heapq.heappop(heap)
        order.append(key)
        if key[0] == "relay":
            out = [("z+" if key[1] % 2 == 0 else "z-", (key[1], 0, 1, 0))]
        elif key[0] == "mirror":
            out = [("x+", ("cen", 1, 0)), ("x-", ("cen", 2, 1)), ("x+", ("cen", 1, 1)), ("x-", ("cen", 2, 0))]
        elif key[0] == "cen":
            out = [("x+" if key[1] == 1 else "x-", ("cen", 3, key[2]))] if key[1:] in ((1, 0), (2, 1)) else []
        else:
            out = sends(key)
        for link, target in out:
            start = max(now, free.get(link, 0.0))
            free[link] = start + cost[link]
            heapq.heappush(heap, (free[link] + lat[link], count, target))
            count += 1
    return order, max(free.values())


def sem_of(key):
    p, dy, dz, dc = key
    return p * 16 + dy * 4 + dz * 2 + dc


def kernel(
    vec_any, sides_ref, cen_any, out_ref,
    vec_ref, cen_ref,
    x_all, xt_all, swap_out, keep_out, relay_x, fin, cen, hn, e_all, m_all, l_all, f_one, den_acc, lse_two, lse_all, lse_sum, num, num_low,
    relay_f32, main_f32, relay_low, main_low, den_out, den_in,
    x_send, x_recv, go_sem, in_sem, r_send, r_recv, f_send, f_recv, c_send, c_recv, l_send, l_recv, n_send, n_recv, d_send, d_recv,
):
    wide = lax.axis_index("wide")
    narrow = lax.axis_index("narrow")
    core = lax.rem(wide, 2)
    z = lax.rem(wide // 2, 8)
    y = lax.rem(narrow // 4, 2) * 2 + wide // 16
    x = lax.rem(narrow, 4)
    zq = z // 4
    rest = lax.rem(z, 4)
    parity = lax.rem(z, 2)
    native = core == rest // 2
    foreign = core != rest // 2
    away = jnp.where(native, 0, 1)
    me = y * 4 + zq * 2 + core

    def device(dx, ny, nz, ncore):
        nx = lax.rem(x + dx + 4, 4)
        return (lax.rem(ny, 2) * 16 + nz * 2 + ncore, (ny // 2) * 4 + nx)

    def up(dy, dz, ncore):
        return device(0, lax.rem(y + dy + 4, 4), lax.rem(z + dz + 8, 8), ncore)

    def peer(index):
        return device(0, index // 4, lax.rem(index // 2, 2) * 4 + rest, lax.rem(index, 2))

    def across(dx):
        return device(dx, y, z, core)

    z_near = z + 1 - 2 * parity
    z_outer = lax.rem(z - 1 + 2 * parity + 8, 8)
    z_second = z + 2 - 4 * (rest // 2)
    near = device(0, y, z_near, 1 - core)
    outer = device(0, y, z_outer, 1 - core)
    second = device(0, y, z_second, core)
    mirror = device(0, y, z_second, 1 - core)

    vec_in = pltpu.make_async_copy(vec_any, vec_ref, in_sem.at[0])
    cen_in = pltpu.make_async_copy(cen_any, cen_ref, in_sem.at[1])
    vec_in.start()
    cen_in.start()
    barrier = pltpu.get_barrier_semaphore()

    around = [up(dy, 0, core) for dy in (1, -1)] + [across(1), across(-1), up(0, 0, 1 - core)]
    around += [up(0, dz, c) for dz in (1, -1) for c in (core, 1 - core)]
    for other in around:
        pl.semaphore_signal(barrier, inc=1, device_id=other, device_id_type=MESH)
    vec_in.wait()
    cen_in.wait()

    first = vec_ref[0:KS, :]
    other_half = vec_ref[KS : 2 * KS, :]
    first_stays = sides_ref[0] == parity
    keep_out[...] = jnp.where(first_stays, first, other_half)
    swap_out[...] = jnp.where(first_stays, other_half, first)
    base = pl.multiple_of(me // 2 * (2 * ROWS) + core * KS, KS)

    @pl.when(native)
    def _():
        x_all[pl.ds(base, KS), :] = keep_out[...]
        cen[0, 0:KS, :] = cen_ref[...]

    pl.semaphore_wait(barrier, len(around))
    for dz in (1, -1):
        pl.semaphore_signal(go_sem, inc=1, device_id=up(0, dz, core), device_id_type=MESH)

    started = []

    def send(src, dst, send_sem, recv_sem, to):
        copy = pltpu.make_async_remote_copy(
            src_ref=src, dst_ref=dst, send_sem=send_sem, recv_sem=recv_sem, device_id=to, device_id_type=MESH
        )
        copy.start()
        started.append(copy)

    def arrived(dst, sem):
        pltpu.make_async_remote_copy(
            src_ref=dst, dst_ref=dst, send_sem=sem, recv_sem=sem, device_id=near, device_id_type=MESH
        ).wait_recv()

    def piece(source, p):
        start = source // 2 * (2 * ROWS) + p // 2 * ROWS + lax.rem(source, 2) * KS + p % 2 * PIECE
        return x_all.at[pl.ds(pl.multiple_of(start, PIECE), PIECE), :]

    def source_of(dy, dz, dc):
        nz = zq if dz == 0 else 1 - zq
        return lax.rem(y - dy + 4, 4) * 4 + nz * 2 + (core if dc == 0 else 1 - core)

    to = tuple(jnp.where(native, a, b) for a, b in zip(near, outer))
    target = (y * 2 + jnp.where(native, zq, z_outer // 4)) * (2 * ROWS) + (1 - core) * KS
    for half in (0, 1):
        send(
            swap_out.at[pl.ds(half * PIECE, PIECE), :],
            x_all.at[pl.ds(pl.multiple_of(target + away * ROWS + half * PIECE, PIECE), PIECE), :],
            x_send.at[half], x_recv.at[(2 * away + half) * 16], to,
        )

    def foreign_rows(half):
        return pltpu.make_async_remote_copy(
            src_ref=keep_out.at[pl.ds(half * PIECE, PIECE), :], dst_ref=piece(me, 2 + half),
            send_sem=f_send.at[half], recv_sem=x_recv.at[(2 + half) * 16], device_id=second, device_id_type=MESH,
        )

    def foreign_centers():
        return pltpu.make_async_remote_copy(
            src_ref=cen_ref, dst_ref=cen.at[0, pl.ds(0, KS), :], send_sem=f_send.at[2], recv_sem=f_recv.at[0],
            device_id=mirror, device_id_type=MESH,
        )

    pl.semaphore_wait(go_sem, 2)

    @pl.when(foreign)
    def _():
        foreign_rows(0).start()
        foreign_rows(1).start()

    def send_centers(it, own):
        for step, slot in ((1, 1), (-1, 2)):
            for half in (0, 1) if step == 1 else (1, 0):
                rows = pl.ds(half * 64, 64)
                index = it * 6 + (slot - 1) * 2 + half
                send(
                    own.at[rows, :], cen.at[it, pl.ds(slot * KS + half * 64, 64), :],
                    c_send.at[index], c_recv.at[index], across(step),
                )

    def relay_center(it, slot, half):
        rows = pl.ds(slot * KS + half * 64, 64)
        arrived(cen.at[it, rows, :], c_recv.at[it * 6 + (slot - 1) * 2 + half])
        index = it * 6 + 4 + half
        send(
            cen.at[it, rows, :], cen.at[it, pl.ds(3 * KS + half * 64, 64), :],
            c_send.at[index], c_recv.at[index], across(1 if slot == 1 else -1),
        )

    def norms(it, q):
        c = cen[it, pl.ds(q * KS, KS), :].astype(F32)
        n = 0.5 * jnp.sum(c * c, axis=1, keepdims=True)
        hn[q] = jnp.broadcast_to(n, (KS, 128))

    def exponents(q, r, product):
        half = hn[q]
        s = (product - jnp.concatenate([half, half], axis=1)) * SCALE
        top = jnp.max(s, axis=0, keepdims=True)
        e = jnp.exp2(s - top)
        e_all[q, r] = e
        m_all[q, pl.ds(r, 1), :] = top
        l_all[q, pl.ds(r, 1), :] = jnp.sum(e, axis=0, keepdims=True)

    def score_chunk(r):
        xt_all[r] = x_all[pl.ds(pl.multiple_of(r * CHUNK, CHUNK), CHUNK), :].T
        for q in range(4):
            exponents(q, r, jnp.dot(cen[0, pl.ds(q * KS, KS), :], xt_all[r], preferred_element_type=F32))

    def score_rows(it, q, count, part):
        def one(g, carry):
            for j in range(UNROLL):
                r = g * UNROLL + j
                product = jnp.dot(
                    cen[it, pl.ds(q * KS, count * KS), :], xt_all[r], preferred_element_type=F32
                )
                for k in range(count):
                    exponents(q + k, r, product[k * KS : (k + 1) * KS, :])
            return carry

        groups = SRC // UNROLL
        first, last = (0, groups) if part is None else (part * groups // 2, (part + 1) * groups // 2)
        lax.fori_loop(first, last, one, 0)

    def score_block(it, q, count=1):
        for k in range(count):
            norms(it, q + k)
        score_rows(it, q, count, None)

    def log_add(parts):
        best = functools.reduce(jnp.maximum, parts)
        return best + jnp.log2(sum(jnp.exp2(part - best) for part in parts))

    def lines(part):
        return slice(0, SRC) if part is None else slice(part * 8, part * 8 + 8)

    def lse_copy(it, part, k):
        other = lax.rem(me // 2 + k, SRC // 2)
        there = lse_all.at[it, me // 2, lines(part), :]
        return pltpu.make_async_remote_copy(
            src_ref=there, dst_ref=there,
            send_sem=l_send.at[it, (part or 0) * 8 + k], recv_sem=l_recv.at[it, (part or 0) * 9 + me // 2],
            device_id=peer(other * 2 + core), device_id_type=MESH,
        )

    def lse_start(it, part):
        at = lines(part)
        tops = [m_all[q, at, :] for q in range(4)]
        top = functools.reduce(jnp.maximum, tops)
        total = sum(l_all[q, at, :] * jnp.exp2(tops[q] - top) for q in range(4))
        lse_two[it, 0, at, :] = top + jnp.log2(total)
        send(
            lse_two.at[it, 0, at, :], lse_two.at[it, 1, at, :],
            l_send.at[it, (part or 0) * 8], l_recv.at[it, (part or 0) * 9 + 8], up(0, 0, 1 - core),
        )

    def lse_tell(it, part):
        at = lines(part)
        arrived(lse_two.at[it, 1, at, :], l_recv.at[it, (part or 0) * 9 + 8])
        lse_all[it, me // 2, at, :] = log_add([lse_two[it, 0, at, :], lse_two[it, 1, at, :]])

        def tell(k, carry):
            lse_copy(it, part, k).start()
            return carry

        lax.fori_loop(1, SRC // 2, tell, 0)

    def lse_hear(it, part):
        at = lines(part)

        def hear(k, carry):
            other = lax.rem(me // 2 + k, SRC // 2)
            arrived(lse_all.at[it, other, at, :], l_recv.at[it, (part or 0) * 9 + other])
            return carry

        lax.fori_loop(1, SRC // 2, hear, 0)
        lse_sum[it, at, :] = log_add([lse_all[it, k, at, :] for k in range(SRC // 2)])

    def weigh(it, q, count=1, late=None):
        blocks = range(count)

        def factors(part):
            at = lines(part)
            for k in blocks:
                f_one[q + k, at, :] = jnp.exp2(m_all[q + k, at, :] - lse_sum[it, at, :])

        factors(None if late is None else 0)

        def group(g, first):
            rolls = []
            for k in blocks:
                parts = []
                den = jnp.zeros((KS, 128), F32)
                for j in range(4):
                    r = g * 4 + j
                    weights = (e_all[q + k, r] * f_one[q + k, pl.ds(r, 1), :]).astype(BF16)
                    wide_weights = weights.astype(F32)
                    den = den + wide_weights[:, :128] + wide_weights[:, 128:]
                    parts.append(weights)
                rolls.append(jnp.concatenate(parts, axis=1))
                den_acc[q + k] = den if first else den_acc[q + k] + den
            rows = x_all[pl.ds(pl.multiple_of(g * 4 * CHUNK, 4 * CHUNK), 4 * CHUNK), :]
            weights = rolls[0] if count == 1 else jnp.concatenate(rolls, axis=0)
            term = jnp.dot(weights, rows, preferred_element_type=F32)
            for k in blocks:
                part = term[k * KS : (k + 1) * KS, :]
                num[it, q + k] = part if first else num[it, q + k] + part

        group(0, True)

        def one(g, carry):
            group(g, False)
            return carry

        if late is None:
            lax.fori_loop(1, 4, one, 0)
        else:
            group(1, False)
            late()
            factors(1)
            lax.fori_loop(2, 4, one, 0)
        here = lax.broadcasted_iota(jnp.int32, (KS, 128), 0) == lax.broadcasted_iota(jnp.int32, (KS, 128), 1)
        for k in blocks:
            column = jnp.sum(den_acc[q + k], axis=1, keepdims=True)
            row = jnp.sum(jnp.where(here, column, 0.0), axis=0, keepdims=True)
            den_out[it, q + k] = jnp.broadcast_to(row, (8, 128))
            if LOW[it] and q + k > 0:
                num_low[it, q + k] = num[it, q + k].astype(BF16)

    def reduce_centers(it, old, late=None):
        table, relay_in, main_in = (num_low, relay_low, main_low) if LOW[it] else (num, relay_f32, main_f32)
        weigh(it, 3, late=late)
        base = it * 6
        for i, (half, step) in enumerate(((0, 1), (1, -1))):
            send(
                table.at[it, 3, pl.ds(half * 64, 64), :], relay_in.at[it, i],
                n_send.at[base + i], n_recv.at[base + i], across(step),
            )
        send(den_out.at[it, 3], den_in.at[it, 3], d_send.at[it * 4 + 3], d_recv.at[it * 4 + 3], across(2))
        weigh(it, 1, 2)
        for i, (q, step, half) in enumerate(((2, 1, 1), (1, -1, 0))):
            send(
                table.at[it, q, pl.ds(half * 64, 64), :], main_in.at[it, i, pl.ds(half * 64, 64), :],
                n_send.at[base + 2 + i], n_recv.at[base + 2 + i], across(step),
            )
            send(den_out.at[it, q], den_in.at[it, 3 - q], d_send.at[it * 4 + q], d_recv.at[it * 4 + 3 - q], across(step))
        for i, (q, step, half) in enumerate(((2, 1, 0), (1, -1, 1))):
            rows = pl.ds(half * 64, 64)
            arrived(relay_in.at[it, i], n_recv.at[base + i])
            part = num[it, q, rows, :] + relay_in[it, i].astype(F32)
            table[it, q, rows, :] = part.astype(table.dtype)
            send(
                table.at[it, q, rows, :], main_in.at[it, i, rows, :],
                n_send.at[base + 4 + i], n_recv.at[base + 4 + i], across(step),
            )
        weigh(it, 0)
        for i, half in enumerate((1, 0)):
            rows = pl.ds(half * 64, 64)
            arrived(main_in.at[it, i, rows, :], n_recv.at[base + 2 + i])
        for k in (1, 2, 3):
            arrived(den_in.at[it, k], d_recv.at[it * 4 + k])
        row = den_out[it, 0] + den_in[it, 1] + den_in[it, 2] + den_in[it, 3]
        here = lax.broadcasted_iota(jnp.int32, (KS, 128), 0) == lax.broadcasted_iota(jnp.int32, (KS, 128), 1)
        column = jnp.sum(jnp.where(here, row[0:1, :], 0.0), axis=1, keepdims=True)
        for i, half in enumerate((0, 1)):
            rows = pl.ds(half * 64, 64)
            arrived(main_in.at[it, i, rows, :], n_recv.at[base + 4 + i])
        total = num[it, 0] + main_in[it, 0].astype(F32) + main_in[it, 1].astype(F32)
        return ((total + old[...].astype(F32)) / (column + 1.0)).astype(BF16)

    order, unused = plan()
    mine = cen.at[0, pl.ds(0, KS), :]
    seen = {}
    ready = []
    blocks = 0
    for number, key in enumerate(order):
        if blocks == 7 and ready:
            score_chunk(ready.pop(0))
        if key[0] == "relay":
            p = key[1]
            step = 2 if p % 2 == 0 else -2
            arrived(relay_x.at[p], r_recv.at[p])
            origin = y * 4 + lax.rem(z - step + 8, 8) // 4 * 2 + core
            send(relay_x.at[p], piece(origin, p), r_send.at[4 + p], x_recv.at[sem_of((p, 0, 1, 0))], up(0, step, core))
            continue
        if key[0] == "mirror":

            @pl.when(foreign)
            def _():
                arrived(mine, f_recv.at[0])

            send_centers(0, mine)
            norms(0, 0)
            blocks += 1
            continue
        if key[0] == "cen":
            slot, half = key[1:]
            rows = pl.ds(slot * KS + half * 64, 64)
            if (slot, half) in ((1, 0), (2, 1)):
                relay_center(0, slot, half)
            else:
                arrived(cen.at[0, rows, :], c_recv.at[(slot - 1) * 2 + half])
            blocks += 1
            if blocks == 7:
                for q in (1, 2, 3):
                    norms(0, q)
            continue
        p, dy, dz, dc = key
        source = source_of(dy, dz, dc)
        if key in ((0, 0, 0, 0), (1, 0, 0, 0)):

            @pl.when(foreign)
            def _():
                arrived(piece(source, p), x_recv.at[sem_of(key)])

        else:
            arrived(piece(source, p), x_recv.at[sem_of(key)])
        for link, goal in sends(key):
            if goal[0] == "relay":
                step = 2 if p % 2 == 0 else -2
                send(piece(source, p), relay_x.at[p], r_send.at[p], r_recv.at[p], up(0, step, core))
            else:
                to = up(0, 0, 1 - core) if link == "c" else up(1 if link == "y+" else -1, 0, core)
                send(piece(source, p), piece(source, p), x_send.at[len(started)], x_recv.at[sem_of(goal)], to)
        if key == MIRROR_AFTER:

            @pl.when(foreign)
            def _():
                foreign_centers().start()

        chunk = (dy, dz, p // 2)
        seen[chunk] = seen.get(chunk, 0) + 1
        if seen[chunk] == PIECES:
            ready.append(source // 2 * 2 + p // 2)
    for r in ready:
        score_chunk(r)
    lse_start(0, None)
    lse_tell(0, None)
    lse_hear(0, None)
    fresh = reduce_centers(0, mine)

    cen[1, 0:KS, :] = fresh
    own = cen.at[1, pl.ds(0, KS), :]
    send_centers(1, own)
    score_block(1, 0)
    relay_center(1, 1, 0)
    relay_center(1, 2, 1)
    for slot in (1, 2):
        half = 2 - slot
        arrived(cen.at[1, pl.ds(slot * KS + half * 64, 64), :], c_recv.at[6 + (slot - 1) * 2 + half])
    score_block(1, 1, 2)
    for half in (0, 1):
        arrived(cen.at[1, pl.ds(3 * KS + half * 64, 64), :], c_recv.at[6 + 4 + half])
    norms(1, 3)
    score_rows(1, 3, 1, 0)
    lse_start(1, 0)
    score_rows(1, 3, 1, 1)
    lse_tell(1, 0)
    lse_start(1, 1)
    lse_tell(1, 1)
    lse_hear(1, 0)
    fin[...] = reduce_centers(1, own, lambda: lse_hear(1, 1))

    @pl.when(native)
    def _():
        out_ref[...] = fin[...]

    @pl.when(foreign)
    def _():
        home = pltpu.make_async_remote_copy(
            src_ref=fin, dst_ref=out_ref, send_sem=f_send.at[3], recv_sem=f_recv.at[1],
            device_id=mirror, device_id_type=MESH,
        )
        home.start()
        home.wait()
        for copy in (foreign_rows(0), foreign_rows(1), foreign_centers()):
            copy.wait_send()

    for copy in started:
        copy.wait_send()
    for it, part in ((0, None), (1, 0), (1, 1)):

        def told(k, carry):
            lse_copy(it, part, k).wait_send()
            return carry

        lax.fori_loop(1, SRC // 2, told, 0)


def local(vectors, block_sides, centers):
    vmem = pltpu.VMEM
    dma = pltpu.SemaphoreType.DMA
    whole = pl.BlockSpec(memory_space=pltpu.VMEM)
    return pl.pallas_call(
        kernel,
        out_shape=jax.ShapeDtypeStruct((KS, D), jnp.bfloat16),
        in_specs=[pl.BlockSpec(memory_space=pl.ANY), pl.BlockSpec(memory_space=pltpu.SMEM), pl.BlockSpec(memory_space=pl.ANY)],
        out_specs=whole,
        scratch_shapes=[
            vmem((2 * KS, D), jnp.bfloat16),
            vmem((KS, D), jnp.bfloat16),
            vmem((SRC * ROWS, D), jnp.bfloat16),
            vmem((SRC, D, CHUNK), jnp.bfloat16),
            vmem((KS, D), jnp.bfloat16),
            vmem((KS, D), jnp.bfloat16),
            vmem((PIECES, PIECE, D), jnp.bfloat16),
            vmem((KS, D), jnp.bfloat16),
            vmem((ITERS, 4 * KS, D), jnp.bfloat16),
            vmem((4, KS, 128), F32),
            vmem((4, SRC, KS, CHUNK), F32),
            vmem((4, SRC, CHUNK), F32),
            vmem((4, SRC, CHUNK), F32),
            vmem((4, SRC, CHUNK), F32),
            vmem((4, KS, 128), F32),
            vmem((ITERS, 2, SRC, CHUNK), F32),
            vmem((ITERS, SRC // 2, SRC, CHUNK), F32),
            vmem((ITERS, SRC, CHUNK), F32),
            vmem((ITERS, 4, KS, D), F32),
            vmem((ITERS, 4, KS, D), BF16),
            vmem((ITERS, 2, 64, D), F32),
            vmem((ITERS, 2, KS, D), F32),
            vmem((ITERS, 2, 64, D), BF16),
            vmem((ITERS, 2, KS, D), BF16),
            vmem((ITERS, 4, 8, 128), F32),
            vmem((ITERS, 4, 8, 128), F32),
            dma((160,)), dma((64,)),
            pltpu.SemaphoreType.REGULAR, dma((2,)),
            dma((8,)), dma((4,)),
            dma((4,)), dma((2,)),
            dma((6 * ITERS,)), dma((6 * ITERS,)),
            dma((ITERS, SRC)), dma((ITERS, 18)),
            dma((6 * ITERS,)), dma((6 * ITERS,)),
            dma((4 * ITERS,)), dma((4 * ITERS,)),
        ],
        compiler_params=pltpu.CompilerParams(
            collective_id=0, has_side_effects=True, vmem_limit_bytes=56 * 1024 * 1024
        ),
        name="refine",
    )(vectors, block_sides, centers)


def solution(mesh):
    in_specs = (P(("wide", "narrow"), None), P(("wide", "narrow")), P(("wide", "narrow"), None))
    out_specs = P(("wide", "narrow"), None)
    return jax.shard_map(local, mesh=mesh, in_specs=in_specs, out_specs=out_specs, check_vma=False)
```
